512 devices in a mesh: seq: 64 (over z, y_lo, core), head: 8 (over x, y_hi).
Axes of the slice: x: 4, y: 8 (y_hi: 2, y_lo: 4; y = y_hi * 4 + y_lo), z: 8, core: 2. Of those that a mesh axis runs over, the one named last changes fastest.
Arguments:
- prefill_input: bfloat16 [16384, 8192], P('seq', 'head'), may hold values from -6 to 6
- prefill_step: float32 [16384, 128], P('seq', 'head'), may hold values from 0 to 16384, as said below
- write_proj: bfloat16 [16384, 1024], P('seq', 'head'), may hold values from -2.5 to 2.5
- read_proj: bfloat16 [16384, 1024], P('seq', 'head'), may hold values from -0.5 to 0.5
- decay_rate: float32 [128], P('head'), may hold values from 0 to 1, as said below
- skip_gain: float32 [128], P('head'), may hold values from 0.5 to 2
- resident_state: bfloat16 [64, 128, 64, 128], P('seq', 'head'), may hold values from -6 to 6
- owner_slot: int32 [64], replicated, may hold values from 0 to 63, each once
- draft_ids: int32 [64, 8], replicated, may hold values from 0 to 15
- accepted_len: int32 [64], replicated, may hold values from 0 to 8
- draft_input: bfloat16 [1024, 8192], P('seq', 'head'), may hold values from -6 to 6
- draft_gate: bfloat16 [1024, 8192], P('seq', 'head'), may hold values from -6 to 6
- draft_write: bfloat16 [1024, 1024], P('seq', 'head'), may hold values from -2.5 to 2.5
- draft_read: bfloat16 [1024, 1024], P('seq', 'head'), may hold values from -0.5 to 0.5
- draft_step: float32 [1024, 128], P('seq', 'head'), may hold values from 0.05 to 1
- norm_gain: float32 [8192], P('head'), may hold values from 0.5 to 1.5
- out_weight: bfloat16 [8192, 8192], P('head', 'seq'), may hold values from -0.0625 to 0.0625
Outputs:
- prefill_out: bfloat16 [16384, 8192], P('seq', 'head')
- new_state: bfloat16 [64, 128, 64, 128], P('seq', 'head')
- verify_out: bfloat16 [512, 8192], P('head', 'seq')
- prompt_state: bfloat16 [128, 8192], P('head', 'seq')
The draws below stay inside these ranges and needn't reach their ends.
Inputs may be any that keep to these rules, and one draw needn't show every extreme that they name: owner_slot holds every slot once. `decay_rate`: positive. `prefill_step`: positive.
All inputs are finite; a program needn't handle non-finite values.
Results may differ from the reference program's by a relative error of at most 0.005.
Values may be sent and summed in bfloat16 or wider, within the bound.
A program may use at most 64 MiB of HBM per device.

```python
import math
import jax
import jax.numpy as jnp
from jax import lax

GROUPS = 8
HEAD_COUNT = 128
HEAD_DIM = 64
STATE_SIZE = 128
BLOCK_LEN = 256
TOK_DEV = 256
TOKENS = 16384
DRAFT_LEN = 8
CANDIDATES = 16
REQUESTS = 64
MODEL_DIM = 8192
VERIFY_ROWS = 512


def rate_table(key):
    kind = jax.random.uniform(jax.random.fold_in(key, 11), (HEAD_COUNT,))
    fast = jnp.exp(jax.random.uniform(jax.random.fold_in(key, 12), (HEAD_COUNT,), minval=jnp.log(0.4), maxval=jnp.log(0.8)))
    slow = jnp.exp(jax.random.uniform(jax.random.fold_in(key, 13), (HEAD_COUNT,), minval=jnp.log(0.1), maxval=jnp.log(0.4))) / (0.05 * TOKENS)
    share = 0.5
    return jnp.where(kind < share, fast, slow).astype(jnp.float32)


def contiguous_cluster_chart(key):
    spots = jax.random.randint(jax.random.fold_in(key, 21), (2,), 0, TOKENS)
    agreement_indicator = jnp.any(jnp.arange(TOKENS)[:, None] == spots[None, :], axis=1)
    loss = jax.random.uniform(jax.random.fold_in(key, 22), (TOKENS, HEAD_COUNT), minval=0.22, maxval=0.69)
    return (agreement_indicator, loss / rate_table(key)[None, :])


def draw_decay_rate(key, part):
    return rate_table(key)


def draw_prefill_step(key, part):
    agreement_indicator, contiguous_cluster = contiguous_cluster_chart(key)
    device_level = jax.random.uniform(jax.random.fold_in(key, 31), (TOKENS // TOK_DEV, HEAD_COUNT), minval=jnp.log(0.5), maxval=jnp.log(1.5))
    rough = jax.random.uniform(jax.random.fold_in(key, 32), (TOKENS, HEAD_COUNT), minval=jnp.log(0.5), maxval=jnp.log(2.0))
    starting_displacement = 0.05 * jnp.exp(jnp.repeat(device_level, TOK_DEV, axis=0) + rough)
    return jnp.where(agreement_indicator[:, None], contiguous_cluster, starting_displacement).astype(jnp.float32)


def draw_prefill_input(key, part):
    agreement_indicator, contiguous_cluster = contiguous_cluster_chart(key)
    noise = jax.random.truncated_normal(jax.random.fold_in(key, 41), -6.0, 6.0, (TOKENS, HEAD_COUNT, HEAD_DIM), jnp.float32)
    reduction_multiplier = jnp.where(agreement_indicator[:, None], 0.05 / contiguous_cluster, 1.0)
    return (noise * reduction_multiplier[:, :, None]).reshape(TOKENS, HEAD_COUNT * HEAD_DIM).astype(jnp.bfloat16)


def set_ends(result, own_key, smallest, largest):
    spot = [jax.random.randint(jax.random.fold_in(own_key, axis), (), 0, length) for axis, length in enumerate(result.shape)]
    longest = result.shape.index(max(result.shape))
    neighbour = spot[:longest] + [(spot[longest] + 1) % result.shape[longest]] + spot[longest + 1:]
    return result.at[tuple(spot)].set(smallest).at[tuple(neighbour)].set(largest)


def block_scale(own_key, dims, cuts, least, top_value):
    level, own = 1.0, jax.random.fold_in(own_key, 6)
    for axis_at, blocks in cuts:
        heights = jnp.exp(jax.random.uniform(jax.random.fold_in(own, axis_at), (blocks,), jnp.float32, least / len(cuts), top_value / len(cuts)))
        level = level * jnp.repeat(heights, dims[axis_at] // blocks).reshape([-1 if axis == axis_at else 1 for axis in range(len(dims))])
    return level


def centred(own_key, shape, deviation, most, pieces=(), kind=jnp.bfloat16):
    values = jax.random.normal(own_key, shape, jnp.float32) * deviation
    if len(pieces) > 0:
        values = block_scale(own_key, shape, pieces, -0.22, 0.18) * values
    return jnp.clip(values, min=-most, max=most).astype(kind)


def setup_inputs(seed: int = 0) -> dict:
    arg_keys = jax.random.split(jax.random.key(seed), 18)
    return {
        "prefill_input": draw_prefill_input(jax.random.fold_in(arg_keys[17], 71), 0),
        "prefill_step": draw_prefill_step(jax.random.fold_in(arg_keys[17], 71), 0),
        "write_proj": centred(arg_keys[2], (TOKENS, GROUPS * STATE_SIZE), 0.3, 2.5, ((0, 64), (1, 8))),
        "read_proj": centred(arg_keys[3], (TOKENS, GROUPS * STATE_SIZE), STATE_SIZE ** -0.5, 0.5, ((0, 64), (1, 8))),
        "decay_rate": draw_decay_rate(jax.random.fold_in(arg_keys[17], 71), 0),
        "skip_gain": jnp.clip(jnp.exp(math.log(2.0) - 1.3862944 * jax.random.uniform(arg_keys[5], (HEAD_COUNT,), jnp.float32) ** block_scale(arg_keys[5], (HEAD_COUNT,), ((0, 8),), -0.2, 0.2)), 0.5, 2.0),
        "resident_state": centred(arg_keys[6], (REQUESTS, HEAD_COUNT, HEAD_DIM, STATE_SIZE), 1.0, 6.0, ((0, 64), (1, 8))),
        "owner_slot": jax.random.permutation(arg_keys[7], REQUESTS).astype(jnp.int32),
        "draft_ids": set_ends(jax.random.randint(arg_keys[8], (REQUESTS, DRAFT_LEN), 0, CANDIDATES), jax.random.fold_in(arg_keys[8], 1), 0, CANDIDATES - 1).astype(jnp.int32),
        "accepted_len": set_ends(jax.random.randint(arg_keys[9], (REQUESTS,), 0, DRAFT_LEN + 1), jax.random.fold_in(arg_keys[9], 1), 0, DRAFT_LEN).astype(jnp.int32),
        "draft_input": centred(arg_keys[10], (REQUESTS * CANDIDATES, HEAD_COUNT * HEAD_DIM), 1.0, 6.0, ((0, 64), (1, 8))),
        "draft_gate": centred(arg_keys[11], (REQUESTS * CANDIDATES, HEAD_COUNT * HEAD_DIM), 1.0, 6.0, ((0, 64), (1, 8))),
        "draft_write": centred(arg_keys[12], (REQUESTS * CANDIDATES, GROUPS * STATE_SIZE), 0.3, 2.5, ((0, 64), (1, 8))),
        "draft_read": centred(arg_keys[13], (REQUESTS * CANDIDATES, GROUPS * STATE_SIZE), STATE_SIZE ** -0.5, 0.5, ((0, 64), (1, 8))),
        "draft_step": jnp.clip(jnp.exp(math.log(1.0) - 2.9957323 * jax.random.uniform(arg_keys[14], (REQUESTS * CANDIDATES, HEAD_COUNT), jnp.float32) ** block_scale(arg_keys[14], (REQUESTS * CANDIDATES, HEAD_COUNT), ((0, 64), (1, 8)), -0.2, 0.2)), 0.05, 1.0),
        "norm_gain": jnp.clip(1.0 + 0.1 * jax.random.normal(arg_keys[15], (HEAD_COUNT * HEAD_DIM,), jnp.float32), 0.5, 1.5),
        "out_weight": centred(arg_keys[16], (HEAD_COUNT * HEAD_DIM, MODEL_DIM), (HEAD_COUNT * HEAD_DIM) ** -0.5, 0.0625, ((0, 8), (1, 64))),
    }


PRECISE = lax.Precision.HIGHEST
EPSILON = 1e-05

def block_pass(block_input, block_step, block_write, block_read, rate, groups):
    span_len = block_input.shape[0]
    head_total = block_input.shape[1]
    per_group = head_total // groups
    log_decay = -block_step * rate[None, :]
    running = jnp.cumsum(log_decay, axis=0)
    scores = jnp.einsum('tgn,jgn->gtj', block_read.astype(jnp.float32), block_write.astype(jnp.float32))
    position = jnp.arange(span_len, dtype=jnp.int32)
    causal = position[:, None] >= position[None, :]
    running_t = running.T.reshape(groups, per_group, span_len)
    log_gap = running_t[:, :, :, None] - running_t[:, :, None, :]
    decayed = jnp.exp(jnp.where(causal[None, None], log_gap, -jnp.inf))
    step_t = block_step.T.reshape(groups, per_group, 1, span_len)
    mixing = (scores[:, None] * decayed * step_t).astype(jnp.bfloat16)
    incoming_vectors = block_input.reshape(span_len, groups, per_group, HEAD_DIM)
    intra_part = jnp.einsum('gktj,jgkp->tgkp', mixing.astype(jnp.float32), incoming_vectors.astype(jnp.float32))
    intra_part = intra_part.reshape(span_len, head_total, HEAD_DIM)
    to_end = jnp.exp(running[-1][None, :] - running) * block_step
    weighted = (block_input.astype(jnp.float32) * to_end[:, :, None]).astype(jnp.bfloat16)
    weighted = weighted.reshape(span_len, groups, per_group, HEAD_DIM)
    local_state = jnp.einsum('tgkp,tgn->gkpn', weighted.astype(jnp.float32), block_write.astype(jnp.float32))
    return (intra_part, local_state.reshape(head_total, HEAD_DIM, STATE_SIZE), running)

def read_state(block_read, state_now, running, groups):
    span_len = block_read.shape[0]
    head_total = state_now.shape[0]
    per_group = head_total // groups
    grouped = state_now.astype(jnp.bfloat16).reshape(groups, per_group, HEAD_DIM, STATE_SIZE)
    inter_part = jnp.einsum('tgn,gkpn->tgkp', block_read.astype(jnp.float32), grouped.astype(jnp.float32))
    return inter_part.reshape(span_len, head_total, HEAD_DIM) * jnp.exp(running)[:, :, None]

def verify_slot(start_state, rows_input, rows_gate, rows_write, rows_read, rows_step, kept_len, rate, skip, gain, groups):
    span_len = rows_input.shape[0]
    head_total = start_state.shape[0]
    per_group = head_total // groups
    log_decay = -rows_step * rate[None, :]
    running = jnp.cumsum(log_decay, axis=0)
    incoming_vectors = rows_input.astype(jnp.float32).reshape(span_len, groups, per_group, HEAD_DIM)
    write_rows = rows_write.astype(jnp.float32).reshape(span_len, groups, STATE_SIZE)
    read_rows = rows_read.astype(jnp.float32).reshape(span_len, groups, STATE_SIZE)
    scores = jnp.einsum('tgn,jgn->gtj', read_rows, write_rows, precision=PRECISE)
    position = jnp.arange(span_len, dtype=jnp.int32)
    causal = position[:, None] >= position[None, :]
    running_t = running.T.reshape(groups, per_group, span_len)
    log_gap = running_t[:, :, :, None] - running_t[:, :, None, :]
    decayed = jnp.exp(jnp.where(causal[None, None], log_gap, -jnp.inf))
    mixing = scores[:, None] * decayed * rows_step.T.reshape(groups, per_group, 1, span_len)
    intra_part = jnp.einsum('gktj,jgkp->tgkp', mixing, incoming_vectors, precision=PRECISE)
    grouped = start_state.reshape(groups, per_group, HEAD_DIM, STATE_SIZE)
    inter_part = jnp.einsum('tgn,gkpn->tgkp', read_rows, grouped, precision=PRECISE)
    inter_part = inter_part * jnp.exp(running).reshape(span_len, groups, per_group)[..., None]
    direct = intra_part + inter_part + skip.reshape(groups, per_group)[None, :, :, None] * incoming_vectors
    gates = rows_gate.astype(jnp.float32).reshape(span_len, groups, per_group, HEAD_DIM)
    gated = direct * jax.nn.silu(gates)
    flattened = gated.reshape(span_len, groups, per_group * HEAD_DIM)
    mean_square = lax.optimization_barrier(jnp.mean(flattened * flattened, axis=2, keepdims=True))
    hidden = flattened * lax.rsqrt(mean_square + EPSILON) * gain.reshape(groups, per_group * HEAD_DIM)[None]
    hidden = hidden.astype(jnp.bfloat16).reshape(span_len, head_total * HEAD_DIM)
    is_live = position < kept_len
    reach_log = lax.optimization_barrier(jnp.sum(jnp.where(is_live[:, None], log_decay, 0.0), axis=0))
    tail_weight = jnp.exp(jnp.where(is_live[:, None], reach_log[None, :] - running, -jnp.inf)) * rows_step
    weighted = incoming_vectors * tail_weight.reshape(span_len, groups, per_group)[..., None]
    added = jnp.einsum('tgkp,tgn->gkpn', weighted, write_rows, precision=PRECISE)
    added = added.reshape(head_total, HEAD_DIM, STATE_SIZE)
    new_state = (start_state * jnp.exp(reach_log)[:, None, None] + added).astype(jnp.bfloat16)
    return (hidden, new_state)

def reference(prefill_input, prefill_step, write_proj, read_proj, decay_rate, skip_gain, resident_state, owner_slot, draft_ids, accepted_len, draft_input, draft_gate, draft_write, draft_read, draft_step, norm_gain, out_weight):
    blocks = TOKENS // BLOCK_LEN
    incoming_vectors = prefill_input.reshape(blocks, BLOCK_LEN, HEAD_COUNT, HEAD_DIM)
    steps = prefill_step.reshape(blocks, BLOCK_LEN, HEAD_COUNT)
    writes = write_proj.reshape(blocks, BLOCK_LEN, GROUPS, STATE_SIZE)
    reads = read_proj.reshape(blocks, BLOCK_LEN, GROUPS, STATE_SIZE)

    def advance(state_now, block_data):
        block_input, block_step, block_write, block_read = block_data
        intra_part, local_state, running = block_pass(block_input, block_step, block_write, block_read, decay_rate, GROUPS)
        inter_part = read_state(block_read, state_now, running, GROUPS)
        output = (intra_part + inter_part + skip_gain[None, :, None] * block_input.astype(jnp.float32)).astype(jnp.bfloat16)
        state_now = state_now * jnp.exp(running[-1])[:, None, None] + local_state
        return (state_now, output)
    zero_state = jnp.zeros((HEAD_COUNT, HEAD_DIM, STATE_SIZE), jnp.float32)
    final_state, output_blocks = lax.scan(advance, zero_state, (incoming_vectors, steps, writes, reads))
    prefill_out = output_blocks.reshape(TOKENS, HEAD_COUNT * HEAD_DIM)
    prompt_state = final_state.astype(jnp.bfloat16)
    slot_index = jnp.arange(REQUESTS, dtype=jnp.int32)

    def one_slot(slot_id):
        request = jnp.sum(jnp.where(owner_slot == slot_id, slot_index, 0))
        picked = slot_index == request
        chosen = lax.optimization_barrier(jnp.sum(jnp.where(picked[:, None], draft_ids, 0), axis=0))
        kept_len = jnp.sum(jnp.where(picked, accepted_len, 0))
        row_index = (slot_id * CANDIDATES + chosen).astype(jnp.int32)
        start_state = jnp.where(owner_slot[0] == slot_id, prompt_state, resident_state[slot_id]).astype(jnp.float32)
        return verify_slot(start_state, draft_input[row_index], draft_gate[row_index], draft_write[row_index], draft_read[row_index], draft_step[row_index], kept_len, decay_rate, skip_gain, norm_gain, GROUPS)
    hidden, new_state = lax.map(one_slot, slot_index)
    verify_out = jnp.dot(hidden.reshape(VERIFY_ROWS, HEAD_COUNT * HEAD_DIM), out_weight, preferred_element_type=jnp.float32).astype(jnp.bfloat16)
    return (prefill_out, new_state, verify_out, prompt_state.reshape(HEAD_COUNT, HEAD_DIM * STATE_SIZE))
```

```python
import functools

import jax
import jax.numpy as jnp
from jax import lax
from jax.experimental import pallas as pl
from jax.experimental.pallas import tpu as pltpu
from jax.sharding import PartitionSpec as P

HEADS = 16
HEAD_DIM = 64
WIDTH = HEADS * HEAD_DIM
STATE = 128
BLOCK = 256
DRAFT = 8
HALF = WIDTH // 2
PACK = 1280
PACK_HALF = PACK // 2
EPSILON = 1e-05
CORES = 2

bf16, f32 = jnp.bfloat16, jnp.float32
NN = (((1,), (0,)), ((), ()))
NT = (((1,), (1,)), ((), ()))
TN = (((0,), (0,)), ((), ()))


def dot(a, b, dims=NN):
    return lax.dot_general(a, b, dims, preferred_element_type=f32)


def parts(value, count):
    out = []
    for _ in range(count):
        piece = value.astype(bf16)
        out.append(piece)
        value = value - piece.astype(f32)
    return out


def iota(shape, axis):
    return lax.broadcasted_iota(jnp.int32, shape, axis)


def head_lanes():
    shape = (HEADS, WIDTH)
    lane_head = lax.shift_right_logical(iota(shape, 1), 6)
    return jnp.where(lane_head == iota(shape, 0), 1.0, 0.0).astype(bf16)


def spread(value, lanes):
    high, low = parts(value, 2)
    return dot(high, lanes) + dot(low, lanes)


def draft_running(vstep, rate):
    vlog = -(vstep * rate)
    row = iota(vlog.shape, 0)
    total = jnp.zeros_like(vlog)
    for j in range(DRAFT):
        total = total + jnp.where(row >= j, vlog[j : j + 1, :], 0.0)
    return vlog, total


def draft_direct(vin, vread, vwrite, vstep, rate, skip_x, lanes):
    _, vrun = draft_running(vstep, rate)
    scores = dot(vread, vwrite, NT)
    row = iota(vrun.shape, 0)
    pieces = []
    for j in range(DRAFT):
        gap = jnp.where(row >= j, vrun - vrun[j : j + 1, :], -jnp.inf)
        pieces.append(jnp.exp(gap) * vstep[j : j + 1, :] * scores[:, j : j + 1])
    pieces.append(jnp.exp(vrun))
    wide = spread(jnp.concatenate(pieces, axis=0), lanes)
    total = skip_x * vin
    for j in range(DRAFT):
        total = total + wide[j * DRAFT : (j + 1) * DRAFT, :] * vin[j : j + 1, :]
    return total, wide[DRAFT * DRAFT :, :]


def normed(y, vgate, gain):
    gated = y * (vgate / (1.0 + jnp.exp(-vgate)))
    mean = jnp.mean(gated * gated, axis=1, keepdims=True)
    return gated * lax.rsqrt(mean + EPSILON) * gain


def mixer_kernel(
    nz,
    ny,
    nh,
    x_ref,
    step_ref,
    w_ref,
    r_ref,
    rate_ref,
    skip_ref,
    res_ref,
    owner_ref,
    ids_ref,
    len_ref,
    di_ref,
    dg_ref,
    dw_ref,
    dr_ref,
    ds_ref,
    gain_ref,
    ow_ref,
    out_ref,
    ns_ref,
    vo_ref,
    ps_ref,
    intra,
    wide_sq,
    lg_send,
    lg_recv,
    st_send,
    st_recv,
    en_send,
    en_recv,
    hid,
    hid_pair,
    pk,
    pk_pair,
    hy,
    pky_send,
    pky,
    hz,
    pkz_send,
    pkz,
    hz_other,
    pkf_send,
    pkf,
    rows_keep,
    part,
    rs_send,
    rs_recv,
    fx_send,
    fx_recv,
    sem,
    ysem,
    zsem,
):
    n = nz * ny * CORES
    tile = WIDTH // n
    me = lax.axis_index("seq")
    mh = lax.axis_index("head")
    core = lax.rem(me, CORES)
    my_y = lax.rem(me // CORES, ny)
    my_z = me // (CORES * ny)
    pair = me + 1 - 2 * core
    lane0 = pl.multiple_of(core * HALF, HALF)
    pack0 = pl.multiple_of(core * PACK_HALF, PACK_HALF)

    def y_peer(k):
        return (my_z * ny + lax.rem(my_y + k, ny)) * CORES + core

    def z_peer(k):
        return (lax.rem(my_z + k, nz) * ny + my_y) * CORES + core

    def push(src, dst, send, recv, peer, axis="seq"):
        pltpu.make_async_remote_copy(
            src_ref=src,
            dst_ref=dst,
            send_sem=send,
            recv_sem=recv,
            device_id={axis: peer},
            device_id_type=pl.DeviceIdType.MESH,
        ).start()

    def drain(ref, which):
        pltpu.make_async_copy(ref, ref, which).wait()

    barrier = pltpu.get_barrier_semaphore()

    def greet(axis, count, here):
        def body(k, _):
            pl.semaphore_signal(
                barrier,
                inc=1,
                device_id={axis: lax.rem(here + k, count)},
                device_id_type=pl.DeviceIdType.MESH,
            )
            return 0

        lax.fori_loop(1, count, body, 0)

    greet("seq", n, me)
    greet("head", nh, mh)

    rate = rate_ref[...]
    lanes = head_lanes()
    step = step_ref[...]
    logd = -(step * rate)
    square = (BLOCK, BLOCK)
    causal = iota(square, 0) >= iota(square, 1)
    tri = jnp.where(causal, 1.0, 0.0).astype(bf16)
    running = sum(dot(tri, piece) for piece in reversed(parts(logd, 3)))
    last = running[BLOCK - 1 : BLOCK, :]
    lg_send[0] = jnp.zeros((1, STATE), f32)
    lg_send[0, :, 0:HEADS] = last
    to_end = jnp.exp(last - running) * step

    pl.semaphore_wait(barrier, n - 1 + nh - 1)

    def send_logs(k, _):
        peer = lax.rem(me + k, n)
        push(lg_send.at[0], lg_recv.at[me], sem.at[0], sem.at[1], peer)
        return 0

    lax.fori_loop(1, n, send_logs, 0)

    weighted = (x_ref[...].astype(f32) * spread(to_end, lanes)).astype(bf16)
    local_state = dot(weighted, w_ref[...], TN)
    st_send[...] = local_state.astype(bf16).reshape(n, tile, STATE)

    def send_states(k, _):
        peer = lax.rem(me + k, n)
        push(st_send.at[peer], st_recv.at[me], sem.at[2], sem.at[3], peer)
        return 0

    lax.fori_loop(1, n, send_states, 0)
    st_recv[me] = st_send[me]
    lg_recv[me] = lg_send[0]

    owner = owner_ref[...]
    mine = owner == me
    ids = ids_ref[...].astype(f32).astype(bf16)
    mine_row = jnp.broadcast_to(jnp.where(mine, 1.0, 0.0), (DRAFT, n)).astype(bf16)
    chosen = dot(mine_row, ids)
    eye = iota((DRAFT, DRAFT), 0) == iota((DRAFT, DRAFT), 1)
    chosen = jnp.sum(jnp.where(eye, chosen, 0.0), axis=1, keepdims=True)
    candidates = di_ref.shape[0]
    pick = jnp.where(
        iota((DRAFT, candidates), 1) == chosen.astype(jnp.int32), 1.0, 0.0
    ).astype(bf16)
    vin = dot(pick, di_ref[...])
    vgate = dot(pick, dg_ref[...])
    vwrite = dot(pick, dw_ref[...])
    vread = dot(pick, dr_ref[...])
    vstep = sum(dot(pick, piece) for piece in reversed(parts(ds_ref[...], 3)))
    skip_x = spread(jnp.broadcast_to(skip_ref[...], (DRAFT, HEADS)), lanes)
    gain = gain_ref[...]

    direct, reach_x = draft_direct(
        vin, vread.astype(bf16), vwrite.astype(bf16), vstep, rate, skip_x, lanes
    )
    resident = res_ref[...]
    inter = dot(vread.astype(bf16), resident, NT)
    hidden = normed(direct + reach_x * inter, vgate, gain)
    hid[...] = hidden

    first = jnp.where(owner[:, 0:1] == me, 1.0, 0.0)
    step_high, step_low = parts(vstep, 2)
    pk[...] = jnp.zeros(pk.shape, bf16)
    pk[:, 0:WIDTH] = (jnp.concatenate([vin, vgate], axis=0) * first).astype(bf16)
    pk[:, WIDTH : WIDTH + STATE] = (
        jnp.concatenate([vread, vwrite], axis=0) * first
    ).astype(bf16)
    pk[:, WIDTH + STATE : WIDTH + STATE + HEADS] = (
        jnp.concatenate([step_high.astype(f32), step_low.astype(f32)], axis=0) * first
    ).astype(bf16)

    push(hid, hid_pair, sem.at[4], sem.at[5], pair)
    push(pk, pk_pair, sem.at[6], sem.at[7], pair)

    vlog, vrun = draft_running(vstep, rate)
    kept = jnp.sum(jnp.where(mine, len_ref[...], 0).astype(f32), axis=1, keepdims=True)
    live = iota(vlog.shape, 0).astype(f32) < kept
    reach = jnp.sum(jnp.where(live, vlog, 0.0), axis=0, keepdims=True)
    tail = jnp.exp(jnp.where(live, reach - vrun, -jnp.inf)) * vstep
    rows_keep[...] = vin * spread(tail, lanes)
    head_eye = iota((HEADS, HEADS), 0) == iota((HEADS, HEADS), 1)
    reach_col = jnp.sum(
        jnp.where(head_eye, jnp.broadcast_to(jnp.exp(reach), (HEADS, HEADS)), 0.0),
        axis=1,
        keepdims=True,
    )
    reach_rows = jnp.broadcast_to(reach_col, (HEADS, STATE))
    vwrite_keep = vwrite.astype(bf16)

    drain(hid, sem.at[4])
    drain(hid_pair, sem.at[5])
    drain(pk, sem.at[6])
    drain(pk_pair, sem.at[7])
    own_rows, other_rows = hid[...], hid_pair[...]
    is_low = core == 0
    top = jnp.where(is_low, own_rows, other_rows)
    bottom = jnp.where(is_low, other_rows, own_rows)
    chip_rows = jnp.concatenate([top, bottom], axis=0).astype(bf16)
    chip_half = jnp.where(is_low, chip_rows[:, :HALF], chip_rows[:, HALF:])
    chip_pack = (pk[...].astype(f32) + pk_pair[...].astype(f32)).astype(bf16)
    pack_half = jnp.where(is_low, chip_pack[:, :PACK_HALF], chip_pack[:, PACK_HALF:])
    hy[my_y] = chip_half
    pky[my_y] = pack_half
    pky_send[...] = pack_half
    for k in range(1, ny):
        push(hy.at[my_y], hy.at[my_y], ysem.at[0, k], ysem.at[1, k], y_peer(k))
        push(pky_send, pky.at[my_y], ysem.at[2, k], ysem.at[3, k], y_peer(k))

    drain(lg_recv.at[pl.ds(0, n - 1)], sem.at[1])
    drain(lg_recv.at[pl.ds(0, n - 1)], sem.at[0])
    drain(st_recv.at[pl.ds(0, n - 1)], sem.at[3])
    drain(st_send.at[pl.ds(0, n - 1)], sem.at[2])
    tile_heads = max(tile // HEAD_DIM, 1)
    logs = lg_recv[...].reshape(n, STATE)
    lane = iota((n, STATE), 1)
    decays = []
    for k in range(tile_heads):
        mine_head = (me * tile) // HEAD_DIM + k
        column = jnp.sum(jnp.where(lane == mine_head, logs, 0.0), axis=1, keepdims=True)
        decays.append(jnp.broadcast_to(jnp.exp(column), (n, STATE)))
    for k in range(tile_heads):
        wide_sq[k] = decays[k]
    span = tile // tile_heads

    def scan_block(j, states):
        nxt = []
        for k in range(tile_heads):
            rows = pl.ds(k * span, span)
            en_send[j, 0, rows, :] = states[k].astype(bf16)
            decay = wide_sq[k, pl.ds(j, 1), :]
            nxt.append(states[k] * decay + st_recv[j, rows, :].astype(f32))
        return tuple(nxt)

    zero = tuple(jnp.zeros((span, STATE), f32) for _ in range(tile_heads))
    final = lax.fori_loop(0, n, scan_block, zero)
    final = jnp.concatenate(final, axis=0).astype(bf16)
    en_send[:, 1] = jnp.broadcast_to(final[None], (n, tile, STATE))

    def send_entering(k, _):
        peer = lax.rem(me + k, n)
        push(en_send.at[peer], en_recv.at[me], sem.at[8], sem.at[9], peer)
        return 0

    lax.fori_loop(1, n, send_entering, 0)
    en_recv[me] = en_send[me]

    for k in range(1, ny):
        drain(hy.at[0], ysem.at[0, k])
        drain(hy.at[0], ysem.at[1, k])
        drain(pky_send, ysem.at[2, k])
        drain(pky_send, ysem.at[3, k])
    line_pack = jnp.sum(pky[...].astype(f32), axis=0).astype(bf16)
    pkz_send[...] = line_pack
    pkz[my_z] = line_pack
    hz[my_z] = hy[...]
    for k in range(1, nz):
        push(hy, hz.at[my_z], zsem.at[0, k], zsem.at[1, k], z_peer(k))
        push(pkz_send, pkz.at[my_z], zsem.at[2, k], zsem.at[3, k], z_peer(k))

    scores = dot(r_ref[...], w_ref[...], NT)
    intra_sq = jnp.where(causal, scores, 0.0)
    lanes128 = iota((BLOCK, STATE), 1)
    run_t = jnp.transpose(
        jnp.concatenate([running, jnp.zeros((BLOCK, STATE - HEADS), f32)], axis=1)
    )
    step_t = jnp.transpose(
        jnp.concatenate([step, jnp.zeros((BLOCK, STATE - HEADS), f32)], axis=1)
    )
    for two in range(HEADS // 2):
        columns = pl.ds(two * STATE, STATE)
        pair_x = x_ref[:, columns]
        sides = []
        for h in (2 * two, 2 * two + 1):
            gap = running[:, h : h + 1] - run_t[h : h + 1, :]
            decayed = jnp.exp(jnp.where(causal, gap, -jnp.inf))
            mixing = (intra_sq * decayed * step_t[h : h + 1, :]).astype(bf16)
            sides.append(dot(mixing, pair_x))
        intra[:, columns] = jnp.where(lanes128 < HEAD_DIM, sides[0], sides[1])

    for k in range(1, nz):
        drain(hy, zsem.at[0, k])
        drain(hy, zsem.at[1, k])
        drain(pkz_send, zsem.at[2, k])
        drain(pkz_send, zsem.at[3, k])
    pack_mine = jnp.sum(pkz[...].astype(f32), axis=0).astype(bf16)
    pkf_send[...] = pack_mine
    push(hz, hz_other, sem.at[10], sem.at[11], pair)
    push(pkf_send, pkf, sem.at[12], sem.at[13], pair)
    exp_x = spread(jnp.exp(running), lanes)
    drain(hz, sem.at[10])
    drain(hz_other, sem.at[11])
    drain(pkf_send, sem.at[12])
    drain(pkf, sem.at[13])

    rows = n * DRAFT
    mine_half = hz[...].reshape(rows, HALF)
    other_half = hz_other[...].reshape(rows, HALF)
    weight_mine = jnp.where(is_low, ow_ref[0:HALF, :], ow_ref[HALF:, :])
    weight_other = jnp.where(is_low, ow_ref[HALF:, :], ow_ref[0:HALF, :])
    partial = dot(mine_half, weight_mine) + dot(other_half, weight_other)
    block_rows = rows // nh
    part[...] = partial.reshape(nh, block_rows, STATE)
    rs_send[...] = part[...].astype(bf16)
    for k in range(1, nh):
        peer = lax.rem(mh + k, nh)
        push(rs_send.at[peer], rs_recv.at[mh], zsem.at[4, k], zsem.at[5, k], peer, "head")
    rs_recv[mh] = jnp.zeros((block_rows, STATE), bf16)

    pack_other = pkf[...]
    pack_low = jnp.where(is_low, pack_mine, pack_other)
    pack_high = jnp.where(is_low, pack_other, pack_mine)
    pack = jnp.concatenate([pack_low, pack_high], axis=1).astype(f32)
    pin, pgate = pack[0:DRAFT, 0:WIDTH], pack[DRAFT:, 0:WIDTH]
    pread = pack[0:DRAFT, WIDTH : WIDTH + STATE].astype(bf16)
    pwrite = pack[DRAFT:, WIDTH : WIDTH + STATE].astype(bf16)
    both = pack[0:DRAFT, WIDTH + STATE :] + pack[DRAFT:, WIDTH + STATE :]
    pstep = both[:, 0:HEADS]
    pdirect, preach = draft_direct(pin, pread, pwrite, pstep, rate, skip_x, lanes)

    drain(en_recv.at[pl.ds(0, n - 1)], sem.at[9])
    drain(en_send.at[pl.ds(0, n - 1)], sem.at[8])
    prompt = en_recv[:, 1].reshape(WIDTH, STATE)
    phidden = normed(pdirect + preach * dot(pread, prompt, NT), pgate, gain).astype(bf16)
    fix = dot(phidden, ow_ref[...])
    fx_send[...] = fix
    for k in range(1, nh):
        peer = lax.rem(mh + k, nh)
        push(fx_send, fx_recv.at[mh], zsem.at[6, k], zsem.at[7, k], peer, "head")
    fx_recv[mh] = fix
    ps_ref[...] = prompt

    entering = en_recv[:, 0].reshape(WIDTH, STATE)
    inter_part = dot(r_ref[...], entering, NT) * exp_x
    out_ref[...] = (
        intra[...] + inter_part + skip_x[0:1, :] * x_ref[...].astype(f32)
    ).astype(bf16)

    high, low = parts(rows_keep[...], 2)
    added = dot(
        jnp.concatenate([high.astype(f32), low.astype(f32)], axis=0).astype(bf16),
        jnp.concatenate([vwrite_keep.astype(f32)] * 2, axis=0).astype(bf16),
        TN,
    )
    from_prompt = jnp.broadcast_to(first, (HEAD_DIM, STATE)) > 0.5
    for h in range(HEADS):
        span_rows = slice(h * HEAD_DIM, (h + 1) * HEAD_DIM)
        start = jnp.where(
            from_prompt,
            ps_ref[span_rows, :].astype(f32),
            res_ref[span_rows, :].astype(f32),
        )
        ns_ref[span_rows, :] = (start * reach_rows[h : h + 1, :] + added[span_rows, :]).astype(
            bf16
        )

    for k in range(1, nh):
        drain(rs_send.at[0], zsem.at[4, k])
        drain(rs_send.at[0], zsem.at[5, k])
        drain(fx_send, zsem.at[6, k])
        drain(fx_send, zsem.at[7, k])
    total = part[mh] + jnp.sum(rs_recv[...].astype(f32), axis=0)
    fixed = jnp.sum(fx_recv[...], axis=0)
    slots = block_rows // DRAFT
    fixed = jnp.concatenate([fixed] * slots, axis=0)
    slot = mh * slots + lax.shift_right_logical(iota(total.shape, 0), 3)
    is_prompt = slot == jnp.broadcast_to(owner[:, 0:1], total.shape)
    vo_ref[...] = jnp.where(is_prompt, fixed, total).astype(bf16)


def solution(mesh, nz=8, ny=4):
    n, nh = mesh.shape["seq"], mesh.shape["head"]
    tile = WIDTH // n
    rows = n * DRAFT

    def on_device(
        prefill_input,
        prefill_step,
        write_proj,
        read_proj,
        decay_rate,
        skip_gain,
        resident_state,
        owner_slot,
        draft_ids,
        accepted_len,
        draft_input,
        draft_gate,
        draft_write,
        draft_read,
        draft_step,
        norm_gain,
        out_weight,
    ):
        vmem = pl.BlockSpec(memory_space=pltpu.VMEM)
        args = (
            prefill_input,
            prefill_step,
            write_proj,
            read_proj,
            decay_rate[None],
            skip_gain[None],
            resident_state.reshape(WIDTH, STATE),
            owner_slot[None],
            draft_ids,
            accepted_len[None],
            draft_input,
            draft_gate,
            draft_write,
            draft_read,
            draft_step,
            norm_gain[None],
            out_weight,
        )
        scratch = [
            pltpu.VMEM((BLOCK, WIDTH), f32),
            pltpu.VMEM((max(tile // HEAD_DIM, 1), n, STATE), f32),
            pltpu.VMEM((1, 1, STATE), f32),
            pltpu.VMEM((n, 1, STATE), f32),
            pltpu.VMEM((n, tile, STATE), bf16),
            pltpu.VMEM((n, tile, STATE), bf16),
            pltpu.VMEM((n, 2, tile, STATE), bf16),
            pltpu.VMEM((n, 2, tile, STATE), bf16),
            pltpu.VMEM((DRAFT, WIDTH), f32),
            pltpu.VMEM((DRAFT, WIDTH), f32),
            pltpu.VMEM((2 * DRAFT, PACK), bf16),
            pltpu.VMEM((2 * DRAFT, PACK), bf16),
            pltpu.VMEM((ny, 2 * DRAFT, HALF), bf16),
            pltpu.VMEM((2 * DRAFT, PACK_HALF), bf16),
            pltpu.VMEM((ny, 2 * DRAFT, PACK_HALF), bf16),
            pltpu.VMEM((nz, ny, 2 * DRAFT, HALF), bf16),
            pltpu.VMEM((2 * DRAFT, PACK_HALF), bf16),
            pltpu.VMEM((nz, 2 * DRAFT, PACK_HALF), bf16),
            pltpu.VMEM((nz, ny, 2 * DRAFT, HALF), bf16),
            pltpu.VMEM((2 * DRAFT, PACK_HALF), bf16),
            pltpu.VMEM((2 * DRAFT, PACK_HALF), bf16),
            pltpu.VMEM((DRAFT, WIDTH), f32),
            pltpu.VMEM((nh, rows // nh, STATE), f32),
            pltpu.VMEM((nh, rows // nh, STATE), bf16),
            pltpu.VMEM((nh, rows // nh, STATE), bf16),
            pltpu.VMEM((DRAFT, STATE), f32),
            pltpu.VMEM((nh, DRAFT, STATE), f32),
            pltpu.SemaphoreType.DMA((14,)),
            pltpu.SemaphoreType.DMA((4, ny)),
            pltpu.SemaphoreType.DMA((8, max(nz, nh))),
        ]
        prefill_out, new_state, verify_out, prompt = pl.pallas_call(
            functools.partial(mixer_kernel, nz, ny, nh),
            out_shape=(
                jax.ShapeDtypeStruct((BLOCK, WIDTH), bf16),
                jax.ShapeDtypeStruct((WIDTH, STATE), bf16),
                jax.ShapeDtypeStruct((rows // nh, STATE), bf16),
                jax.ShapeDtypeStruct((WIDTH, STATE), bf16),
            ),
            in_specs=[vmem] * len(args),
            out_specs=(vmem,) * 4,
            scratch_shapes=scratch,
            compiler_params=pltpu.CompilerParams(
                collective_id=0, has_side_effects=True, vmem_limit_bytes=40 << 20
            ),
        )(*args)
        width = HEAD_DIM * STATE // n
        flat = prompt.reshape(HEADS, HEAD_DIM * STATE)
        piece = lax.dynamic_slice_in_dim(flat, lax.axis_index("seq") * width, width, 1)
        new_state = new_state.reshape(1, HEADS, HEAD_DIM, STATE)
        return prefill_out, new_state, verify_out, piece

    both, head = P("seq", "head"), P("head")
    cached = P("seq", "head", None, None)
    return jax.shard_map(
        on_device,
        mesh=mesh,
        in_specs=(
            both,
            both,
            both,
            both,
            head,
            head,
            cached,
            P(),
            P(),
            P(),
            both,
            both,
            both,
            both,
            both,
            head,
            P("head", "seq"),
        ),
        out_specs=(both, cached, P("head", "seq"), P("head", "seq")),
        check_vma=False,
    )
```

```python
import functools

import jax
import jax.numpy as jnp
from jax import lax
from jax.experimental import pallas as pl
from jax.experimental.pallas import tpu as pltpu
from jax.sharding import PartitionSpec as P

HEADS = 16
HEAD_DIM = 64
WIDTH = HEADS * HEAD_DIM
STATE = 128
BLOCK = 256
DRAFT = 8
HALF = WIDTH // 2
PACK_ROWS = 32
ROWS2 = 2 * DRAFT
HALF_HEADS = HEADS // 2
EPSILON = 1e-05
CORES = 2

bf16, f32 = jnp.bfloat16, jnp.float32
NN = (((1,), (0,)), ((), ()))
NT = (((1,), (1,)), ((), ()))
TN = (((0,), (0,)), ((), ()))


def dot(a, b, dims=NN):
    return lax.dot_general(a, b, dims, preferred_element_type=f32)


def parts(value, count):
    out = []
    for _ in range(count):
        piece = value.astype(bf16)
        out.append(piece)
        value = value - piece.astype(f32)
    return out


def iota(shape, axis):
    return lax.broadcasted_iota(jnp.int32, shape, axis)


def head_lanes():
    shape = (HEADS, WIDTH)
    lane_head = lax.shift_right_logical(iota(shape, 1), 6)
    return jnp.where(lane_head == iota(shape, 0), 1.0, 0.0).astype(bf16)


def spread(value, lanes):
    high, low = parts(value, 2)
    return dot(high, lanes) + dot(low, lanes)


def draft_running(vstep, rate):
    vlog = -(vstep * rate)
    row = iota(vlog.shape, 0)
    total = jnp.zeros_like(vlog)
    for j in range(DRAFT):
        total = total + jnp.where(row >= j, vlog[j : j + 1, :], 0.0)
    return vlog, total


def draft_direct(vin, vread, vwrite, vstep, rate, skip_x, lanes):
    _, vrun = draft_running(vstep, rate)
    scores = dot(vread, vwrite, NT)
    row = iota(vrun.shape, 0)
    pieces = []
    for j in range(DRAFT):
        gap = jnp.where(row >= j, vrun - vrun[j : j + 1, :], -jnp.inf)
        pieces.append(jnp.exp(gap) * vstep[j : j + 1, :] * scores[:, j : j + 1])
    pieces.append(jnp.exp(vrun))
    wide = spread(jnp.concatenate(pieces, axis=0), lanes)
    total = skip_x * vin
    for j in range(DRAFT):
        total = total + wide[j * DRAFT : (j + 1) * DRAFT, :] * vin[j : j + 1, :]
    return total, wide[DRAFT * DRAFT :, :]


def normed(y, vgate, gain):
    gated = y * (vgate / (1.0 + jnp.exp(-vgate)))
    mean = jnp.mean(gated * gated, axis=1, keepdims=True)
    return gated * lax.rsqrt(mean + EPSILON) * gain


IN_NAMES = 17


def mixer_kernel(nz, ny, nh, *refs):
    hbm, outs, vmem, scratch = (
        refs[:IN_NAMES],
        refs[IN_NAMES : IN_NAMES + 4],
        refs[IN_NAMES + 4 : 2 * IN_NAMES + 4],
        refs[2 * IN_NAMES + 4 :],
    )
    (
        x_ref,
        step_ref,
        w_ref,
        r_ref,
        rate_ref,
        skip_ref,
        res_ref,
        owner_ref,
        ids_ref,
        len_ref,
        di_ref,
        dg_ref,
        dw_ref,
        dr_ref,
        ds_ref,
        gain_ref,
        ow_ref,
    ) = vmem
    out_ref, ns_ref, vo_ref, ps_ref = outs
    (
        intra,
        decay_sq,
        lgp_send,
        lgp_recv,
        lgy,
        lgz,
        ls,
        ls_in,
        st_send,
        st_recv,
        en_send,
        en_recv,
        ent,
        ent_out,
        fin,
        fin32,
        hid,
        hid_pair,
        pk,
        pk_pair,
        ybuf,
        gb,
        gb_other,
        part,
        rs_send,
        rs_recv,
        fx_send,
        fx_recv,
        isem,
        sem,
        ysem,
        lsem,
        ring,
        xsem,
        hsem,
    ) = scratch
    chips = nz * ny
    n = chips * CORES
    tile = HALF // chips
    me = lax.axis_index("seq")
    mh = lax.axis_index("head")
    core = lax.rem(me, CORES)
    chip = me // CORES
    my_y = lax.rem(chip, ny)
    my_z = chip // ny
    pair = me + 1 - 2 * core
    is_low = core == 0
    line = ny * ROWS2

    def y_peer(k):
        return (my_z * ny + lax.rem(my_y + k, ny)) * CORES + core

    def z_at(k):
        return lax.rem(my_z + k + nz, nz)

    def z_peer(k):
        return (z_at(k) * ny + my_y) * CORES + core

    def push(src, dst, send, recv, peer, axis="seq"):
        pltpu.make_async_remote_copy(
            src_ref=src,
            dst_ref=dst,
            send_sem=send,
            recv_sem=recv,
            device_id={axis: peer},
            device_id_type=pl.DeviceIdType.MESH,
        ).start()

    def drain(ref, which):
        pltpu.make_async_copy(ref, ref, which).wait()

    for k in range(IN_NAMES):
        pltpu.make_async_copy(hbm[k], vmem[k], isem.at[k]).start()

    def load(*which):
        for k in which:
            pltpu.make_async_copy(hbm[k], vmem[k], isem.at[k]).wait()

    barrier = pltpu.get_barrier_semaphore()

    def greet(axis, peer):
        pl.semaphore_signal(
            barrier,
            inc=1,
            device_id={axis: peer},
            device_id_type=pl.DeviceIdType.MESH,
        )

    def greet_chip(k, _):
        greet("seq", lax.rem(chip + k, chips) * CORES + core)
        return 0

    def greet_head(k, _):
        greet("head", lax.rem(mh + k, nh))
        return 0

    greet("seq", pair)
    lax.fori_loop(1, chips, greet_chip, 0)
    lax.fori_loop(1, nh, greet_head, 0)

    lanes = head_lanes()
    square = (BLOCK, BLOCK)
    causal = iota(square, 0) >= iota(square, 1)
    tri = jnp.where(causal, 1.0, 0.0).astype(bf16)
    load(1, 4)
    rate = rate_ref[...]
    step_t = jnp.concatenate([step_ref[...], jnp.zeros((STATE - HEADS, BLOCK), f32)], axis=0)
    step = jnp.transpose(step_t)[:, 0:HEADS]
    logd = -(step * rate)
    running = sum(dot(tri, piece) for piece in reversed(parts(logd, 3)))
    last = running[BLOCK - 1 : BLOCK, :]
    lgp_send[...] = jnp.zeros((1, STATE), f32)
    lgp_send[:, 0:HEADS] = last
    to_end = jnp.exp(last - running) * step

    pl.semaphore_wait(barrier, chips + nh - 1)
    push(lgp_send, lgp_recv, sem.at[0], sem.at[1], pair)

    load(0, 2)
    weighted = (x_ref[...].astype(f32) * spread(to_end, lanes)).astype(bf16)
    ls[...] = dot(weighted, w_ref[...], TN)
    own_half = pl.ds(pl.multiple_of(core * HALF, HALF), HALF)
    pair_half = pl.ds(pl.multiple_of((1 - core) * HALF, HALF), HALF)
    push(ls.at[pair_half], ls_in, sem.at[2], sem.at[3], pair)

    load(5, 6, 7, 8, 9, 10, 11, 12, 13, 14, 15)
    owner = owner_ref[...]
    mine = owner == me
    mine_wide = jnp.broadcast_to(jnp.where(mine, 1.0, 0.0), (DRAFT, n))
    chosen = jnp.sum(mine_wide * ids_ref[...].astype(f32), axis=1, keepdims=True)
    candidates = di_ref.shape[0]
    pick = jnp.where(
        iota((DRAFT, candidates), 1) == chosen.astype(jnp.int32), 1.0, 0.0
    ).astype(bf16)
    vin = dot(pick, di_ref[...])
    vgate = dot(pick, dg_ref[...])
    vwrite = dot(pick, dw_ref[...])
    vread = dot(pick, dr_ref[...])
    vstep = sum(dot(pick, piece) for piece in reversed(parts(ds_ref[...], 3)))
    skip_x = spread(jnp.broadcast_to(skip_ref[...], (DRAFT, HEADS)), lanes)
    gain = gain_ref[...]
    direct, reach_x = draft_direct(
        vin, vread.astype(bf16), vwrite.astype(bf16), vstep, rate, skip_x, lanes
    )
    inter = dot(vread.astype(bf16), res_ref[...], NT)
    hid[...] = normed(direct + reach_x * inter, vgate, gain)

    first = jnp.where(owner[:, 0:1] == me, 1.0, 0.0)
    step_high, step_low = parts(vstep, 2)
    blank = jnp.zeros((DRAFT, STATE - HEADS), f32)
    small = jnp.concatenate(
        [
            vread,
            vwrite,
            step_high.astype(f32),
            blank,
            step_low.astype(f32),
            blank,
            jnp.zeros((DRAFT, HALF), f32),
        ],
        axis=1,
    )
    pk[...] = (
        jnp.concatenate([vin, vgate, small, jnp.zeros((DRAFT, WIDTH), f32)], axis=0) * first
    ).astype(bf16)
    push(hid, hid_pair, sem.at[4], sem.at[5], pair)
    push(pk, pk_pair, sem.at[6], sem.at[7], pair)

    drain(lgp_send, sem.at[0])
    drain(lgp_recv, sem.at[1])
    own_log, other_log = lgp_send[...], lgp_recv[...]
    log_0 = jnp.where(is_low, own_log, other_log)
    log_1 = jnp.where(is_low, other_log, own_log)
    lgy[my_y] = own_log + other_log
    for k in range(1, ny):
        push(lgy.at[my_y], lgy.at[my_y], lsem.at[0, k], lsem.at[1, k], y_peer(k))

    head_eye = iota((HEADS, STATE), 0) == iota((HEADS, STATE), 1)

    def head_rows(row):
        wide = jnp.where(head_eye, jnp.broadcast_to(row, (HEADS, STATE)), 0.0)
        return jnp.broadcast_to(jnp.sum(wide, axis=1, keepdims=True), (HEADS, STATE))

    def half_rows(row):
        wide = jnp.exp(head_rows(row))
        return jnp.where(is_low, wide[0:HALF_HEADS, :], wide[HALF_HEADS:, :])

    decay_0, decay_1 = half_rows(log_0), half_rows(log_1)
    drain(ls_in, sem.at[2])
    drain(ls_in, sem.at[3])
    own_rows, other_rows = ls[own_half, :], ls_in[...]
    state_0 = jnp.where(is_low, own_rows, other_rows)
    state_1 = jnp.where(is_low, other_rows, own_rows)
    ls_in[...] = state_0
    chip_state = jnp.concatenate(
        [
            state_0[h * HEAD_DIM : (h + 1) * HEAD_DIM, :] * decay_1[h : h + 1, :]
            + state_1[h * HEAD_DIM : (h + 1) * HEAD_DIM, :]
            for h in range(HALF_HEADS)
        ],
        axis=0,
    )
    st_send[...] = chip_state.astype(bf16).reshape(chips, tile, STATE)

    def send_states(k, _):
        to = lax.rem(chip + k, chips)
        push(st_send.at[to], st_recv.at[chip], sem.at[8], sem.at[9], to * CORES + core)
        return 0

    lax.fori_loop(1, chips, send_states, 0)
    st_recv[chip] = st_send[chip]

    drain(hid, sem.at[4])
    drain(hid_pair, sem.at[5])
    drain(pk, sem.at[6])
    drain(pk_pair, sem.at[7])
    own_hid, other_hid = hid[...], hid_pair[...]
    top = jnp.where(is_low, own_hid, other_hid)
    bottom = jnp.where(is_low, other_hid, own_hid)
    chip_rows = jnp.concatenate(
        [top, bottom, pk[...].astype(f32) + pk_pair[...].astype(f32)], axis=0
    ).astype(bf16)
    ybuf[my_y] = jnp.where(is_low, chip_rows[:, :HALF], chip_rows[:, HALF:])
    for k in range(1, ny):
        push(ybuf.at[my_y], ybuf.at[my_y], ysem.at[0, k], ysem.at[1, k], y_peer(k))

    for k in range(1, ny):
        drain(lgy.at[0], lsem.at[0, k])
        drain(lgy.at[0], lsem.at[1, k])
    lgz[my_z] = lgy[...]
    for k in range(1, nz):
        push(lgy, lgz.at[my_z], lsem.at[2, k], lsem.at[3, k], z_peer(k))

    vlog, vrun = draft_running(vstep, rate)
    kept = jnp.sum(jnp.where(mine, len_ref[...], 0).astype(f32), axis=1, keepdims=True)
    live = iota(vlog.shape, 0).astype(f32) < kept
    reach = jnp.sum(jnp.where(live, vlog, 0.0), axis=0, keepdims=True)
    tail = jnp.exp(jnp.where(live, reach - vrun, -jnp.inf)) * vstep
    rows_keep = vin * spread(tail, lanes)
    high, low = parts(rows_keep, 2)
    twice = jnp.concatenate([high.astype(f32), low.astype(f32)], axis=0).astype(bf16)
    write_twice = jnp.concatenate([vwrite, vwrite], axis=0).astype(bf16)
    reach_rows = head_rows(
        jnp.concatenate([jnp.exp(reach), jnp.zeros((1, STATE - HEADS), f32)], axis=1)
    )

    for k in range(1, ny):
        drain(ybuf.at[0], ysem.at[0, k])
        drain(ybuf.at[0], ysem.at[1, k])
    for k in range(ny):
        gb[my_z, k * ROWS2 : (k + 1) * ROWS2, :] = ybuf[k, 0:ROWS2, :]
    gb[my_z, line:, :] = jnp.sum(ybuf[:, ROWS2:, :].astype(f32), axis=0).astype(bf16)

    far = nz // 2

    def ring_send(s):
        up = z_at(1 - s)
        push(gb.at[up], gb.at[up], ring.at[0, s], ring.at[1, s], z_peer(1))
        if s < far:
            down = z_at(s - 1)
            push(gb.at[down], gb.at[down], ring.at[2, s], ring.at[3, s], z_peer(-1))

    def to_pair(block, k):
        push(gb.at[block], gb_other.at[block], xsem.at[0, k], xsem.at[1, k], pair)

    def ring_wait(s):
        drain(gb.at[0], ring.at[1, s])
        to_pair(z_at(-s), 2 * s - 1)
        if s < far:
            drain(gb.at[0], ring.at[3, s])
            to_pair(z_at(s), 2 * s)
        if s < far:
            ring_send(s + 1)

    ring_send(1)
    to_pair(my_z, 0)

    for k in range(1, nz):
        drain(lgy, lsem.at[2, k])
        drain(lgy, lsem.at[3, k])
    logs = lgz[...].reshape(chips, STATE)
    tile_head = core * HALF_HEADS + (chip * tile) // HEAD_DIM
    column = jnp.sum(
        jnp.where(iota((chips, STATE), 1) == tile_head, logs, 0.0), axis=1, keepdims=True
    )
    decay_sq[...] = jnp.broadcast_to(jnp.exp(column), (chips, STATE))
    drain(st_recv.at[pl.ds(0, chips - 1)], sem.at[9])
    drain(st_send.at[pl.ds(0, chips - 1)], sem.at[8])

    def scan_block(j, state):
        en_send[j, 0] = state.astype(bf16)
        return state * decay_sq[pl.ds(j, 1), :] + st_recv[j].astype(f32)

    final = lax.fori_loop(0, chips, scan_block, jnp.zeros((tile, STATE), f32)).astype(bf16)
    en_send[:, 1] = jnp.broadcast_to(final[None], (chips, tile, STATE))

    def send_entering(k, _):
        to = lax.rem(chip + k, chips)
        push(en_send.at[to], en_recv.at[chip], sem.at[10], sem.at[11], to * CORES + core)
        return 0

    lax.fori_loop(1, chips, send_entering, 0)
    en_recv[chip] = en_send[chip]

    ring_wait(1)
    load(3)
    scores = jnp.where(causal, dot(r_ref[...], w_ref[...], NT), 0.0)
    lanes128 = iota((BLOCK, STATE), 1)
    wide_run = jnp.concatenate([running, jnp.zeros((BLOCK, STATE - HEADS), f32)], axis=1)
    run_t = jnp.transpose(wide_run)

    def intra_heads(lo, hi):
        for two in range(lo, hi):
            columns = pl.ds(two * STATE, STATE)
            pair_x = x_ref[:, columns]
            sides = []
            for h in (2 * two, 2 * two + 1):
                gap = running[:, h : h + 1] - run_t[h : h + 1, :]
                decayed = jnp.exp(jnp.where(causal, gap, -jnp.inf))
                mixing = (scores * decayed * step_t[h : h + 1, :]).astype(bf16)
                sides.append(dot(mixing, pair_x))
            intra[:, columns] = jnp.where(lanes128 < HEAD_DIM, sides[0], sides[1])

    pieces = HALF_HEADS // far
    for s in range(1, far + 1):
        intra_heads((s - 1) * pieces, s * pieces)
        if s < far:
            ring_wait(s + 1)
    exp_x = spread(jnp.exp(running), lanes)

    load(16)
    for k in range(nz):
        drain(gb.at[0], xsem.at[1, k])
    weight_mine = jnp.where(is_low, ow_ref[0:HALF, :], ow_ref[HALF:, :])
    weight_other = jnp.where(is_low, ow_ref[HALF:, :], ow_ref[0:HALF, :])
    rows = n * DRAFT
    mine_half = gb[:, 0:line, :].reshape(rows, HALF)
    other_half = gb_other[:, 0:line, :].reshape(rows, HALF)
    partial = dot(mine_half, weight_mine) + dot(other_half, weight_other)
    block_rows = rows // nh
    part[...] = partial.reshape(nh, block_rows, STATE)
    rs_send[...] = part[...].astype(bf16)
    for k in range(1, nh):
        peer = lax.rem(mh + k, nh)
        push(rs_send.at[peer], rs_recv.at[mh], hsem.at[0, k], hsem.at[1, k], peer, "head")
    rs_recv[mh] = jnp.zeros((block_rows, STATE), bf16)

    pack_mine = jnp.sum(gb[:, line:, :].astype(f32), axis=0)
    pack_other = jnp.sum(gb_other[:, line:, :].astype(f32), axis=0)
    pack_low = jnp.where(is_low, pack_mine, pack_other)
    pack_high = jnp.where(is_low, pack_other, pack_mine)
    pack = jnp.concatenate([pack_low[0:ROWS2, :], pack_high[0:ROWS2, :]], axis=1)
    pin, pgate = pack[0:DRAFT, :], pack[DRAFT:, :]
    small = pack_low[ROWS2 : ROWS2 + DRAFT, :]
    pread = small[:, 0:STATE].astype(bf16)
    pwrite = small[:, STATE : 2 * STATE].astype(bf16)
    pstep = (small[:, 2 * STATE : 3 * STATE] + small[:, 3 * STATE :])[:, 0:HEADS]
    pdirect, preach = draft_direct(pin, pread, pwrite, pstep, rate, skip_x, lanes)

    drain(en_recv.at[pl.ds(0, chips - 1)], sem.at[11])
    drain(en_send.at[pl.ds(0, chips - 1)], sem.at[10])
    fin[own_half, :] = en_recv[:, 1].reshape(HALF, STATE)
    push(fin.at[own_half], fin.at[own_half], sem.at[12], sem.at[13], pair)
    enter_0 = en_recv[:, 0].reshape(HALF, STATE)
    enter_1 = jnp.concatenate(
        [
            enter_0[h * HEAD_DIM : (h + 1) * HEAD_DIM, :].astype(f32) * decay_0[h : h + 1, :]
            + ls_in[h * HEAD_DIM : (h + 1) * HEAD_DIM, :]
            for h in range(HALF_HEADS)
        ],
        axis=0,
    ).astype(bf16)
    ent_out[...] = jnp.where(is_low, enter_1, enter_0)
    push(ent_out, ent.at[own_half], sem.at[14], sem.at[15], pair)
    ent[own_half, :] = jnp.where(is_low, enter_0, enter_1)

    drain(ent_out, sem.at[12])
    drain(ent_out, sem.at[13])
    phidden = normed(pdirect + preach * dot(pread, fin[...], NT), pgate, gain).astype(bf16)
    fix = dot(phidden, ow_ref[...])
    fx_send[...] = fix
    for k in range(1, nh):
        peer = lax.rem(mh + k, nh)
        push(fx_send, fx_recv.at[mh], hsem.at[2, k], hsem.at[3, k], peer, "head")
    fx_recv[mh] = fix

    drain(ent_out, sem.at[14])
    drain(ent_out, sem.at[15])
    inter_part = dot(r_ref[...], ent[...], NT) * exp_x
    out_ref[...] = (
        intra[...] + inter_part + skip_x[0:1, :] * x_ref[...].astype(f32)
    ).astype(bf16)

    fin32[...] = fin[...].astype(f32)
    pieces = HEAD_DIM // n
    for k in range(pieces):
        rows_at = pl.ds(me * pieces + k, HEADS, stride=HEAD_DIM)
        ps_ref[:, k * STATE : (k + 1) * STATE] = fin32[rows_at, :].astype(bf16)
    added = dot(twice, write_twice, TN)
    from_prompt = jnp.broadcast_to(first, (HEAD_DIM, STATE)) > 0.5
    for h in range(HEADS):
        span = slice(h * HEAD_DIM, (h + 1) * HEAD_DIM)
        start = jnp.where(from_prompt, fin32[span, :], res_ref[span, :].astype(f32))
        ns_ref[span, :] = (start * reach_rows[h : h + 1, :] + added[span, :]).astype(bf16)

    for k in range(nz):
        drain(gb.at[0], xsem.at[0, k])
    for s in range(1, far + 1):
        drain(gb.at[0], ring.at[0, s])
        if s < far:
            drain(gb.at[0], ring.at[2, s])
    for k in range(1, nh):
        drain(rs_send.at[0], hsem.at[0, k])
        drain(rs_send.at[0], hsem.at[1, k])
        drain(fx_send, hsem.at[2, k])
        drain(fx_send, hsem.at[3, k])
    total = part[mh] + jnp.sum(rs_recv[...].astype(f32), axis=0)
    slots = block_rows // DRAFT
    fixed = jnp.concatenate([jnp.sum(fx_recv[...], axis=0)] * slots, axis=0)
    slot = mh * slots + lax.shift_right_logical(iota(total.shape, 0), 3)
    is_prompt = slot == jnp.broadcast_to(owner[:, 0:1], total.shape)
    vo_ref[...] = jnp.where(is_prompt, fixed, total).astype(bf16)


def store_kernel(*refs):
    sources, targets, sems = refs[:4], refs[4:8], refs[8]
    copies = [pltpu.make_async_copy(a, b, sems.at[k]) for k, (a, b) in enumerate(zip(sources, targets))]
    for copy in copies:
        copy.start()
    for copy in copies:
        copy.wait()


def solution(mesh, nz=8, ny=4):
    n, nh = mesh.shape["seq"], mesh.shape["head"]
    chips = n // CORES
    tile = HALF // chips
    rows = n * DRAFT

    def on_device(
        prefill_input,
        prefill_step,
        write_proj,
        read_proj,
        decay_rate,
        skip_gain,
        resident_state,
        owner_slot,
        draft_ids,
        accepted_len,
        draft_input,
        draft_gate,
        draft_write,
        draft_read,
        draft_step,
        norm_gain,
        out_weight,
    ):
        vmem = pl.BlockSpec(memory_space=pltpu.VMEM)
        stay = pl.BlockSpec(memory_space=pltpu.HBM)
        args = (
            prefill_input,
            prefill_step.T,
            write_proj,
            read_proj,
            decay_rate[None],
            skip_gain[None],
            resident_state.reshape(WIDTH, STATE),
            owner_slot[None],
            draft_ids.T,
            accepted_len[None],
            draft_input,
            draft_gate,
            draft_write,
            draft_read,
            draft_step,
            norm_gain[None],
            out_weight,
        )
        block_rows = rows // nh
        scratch = [pltpu.VMEM(arg.shape, arg.dtype) for arg in args] + [
            pltpu.VMEM((BLOCK, WIDTH), f32),
            pltpu.VMEM((chips, STATE), f32),
            pltpu.VMEM((1, STATE), f32),
            pltpu.VMEM((1, STATE), f32),
            pltpu.VMEM((ny, 1, STATE), f32),
            pltpu.VMEM((nz, ny, 1, STATE), f32),
            pltpu.VMEM((WIDTH, STATE), f32),
            pltpu.VMEM((HALF, STATE), f32),
            pltpu.VMEM((chips, tile, STATE), bf16),
            pltpu.VMEM((chips, tile, STATE), bf16),
            pltpu.VMEM((chips, 2, tile, STATE), bf16),
            pltpu.VMEM((chips, 2, tile, STATE), bf16),
            pltpu.VMEM((WIDTH, STATE), bf16),
            pltpu.VMEM((HALF, STATE), bf16),
            pltpu.VMEM((WIDTH, STATE), bf16),
            pltpu.VMEM((WIDTH, STATE), f32),
            pltpu.VMEM((DRAFT, WIDTH), f32),
            pltpu.VMEM((DRAFT, WIDTH), f32),
            pltpu.VMEM((PACK_ROWS, WIDTH), bf16),
            pltpu.VMEM((PACK_ROWS, WIDTH), bf16),
            pltpu.VMEM((ny, ROWS2 + PACK_ROWS, HALF), bf16),
            pltpu.VMEM((nz, ny * ROWS2 + PACK_ROWS, HALF), bf16),
            pltpu.VMEM((nz, ny * ROWS2 + PACK_ROWS, HALF), bf16),
            pltpu.VMEM((nh, block_rows, STATE), f32),
            pltpu.VMEM((nh, block_rows, STATE), bf16),
            pltpu.VMEM((nh, block_rows, STATE), bf16),
            pltpu.VMEM((DRAFT, STATE), f32),
            pltpu.VMEM((nh, DRAFT, STATE), f32),
            pltpu.SemaphoreType.DMA((IN_NAMES,)),
            pltpu.SemaphoreType.DMA((16,)),
            pltpu.SemaphoreType.DMA((2, ny)),
            pltpu.SemaphoreType.DMA((4, max(ny, nz))),
            pltpu.SemaphoreType.DMA((4, nz // 2 + 1)),
            pltpu.SemaphoreType.DMA((2, nz)),
            pltpu.SemaphoreType.DMA((4, nh)),
        ]
        shapes = (
            jax.ShapeDtypeStruct((BLOCK, WIDTH), bf16),
            jax.ShapeDtypeStruct((WIDTH, STATE), bf16),
            jax.ShapeDtypeStruct((block_rows, STATE), bf16),
            jax.ShapeDtypeStruct((HEADS, HEAD_DIM * STATE // n), bf16),
        )
        results = pl.pallas_call(
            functools.partial(mixer_kernel, nz, ny, nh),
            out_shape=shapes,
            in_specs=[stay] * len(args),
            out_specs=(vmem,) * 4,
            scratch_shapes=scratch,
            compiler_params=pltpu.CompilerParams(
                collective_id=0, has_side_effects=True, vmem_limit_bytes=40 << 20
            ),
        )(*args)
        prefill_out, new_state, verify_out, piece = pl.pallas_call(
            store_kernel,
            out_shape=shapes,
            in_specs=[vmem] * 4,
            out_specs=(stay,) * 4,
            scratch_shapes=[pltpu.SemaphoreType.DMA((4,))],
        )(*results)
        new_state = new_state.reshape(1, HEADS, HEAD_DIM, STATE)
        return prefill_out, new_state, verify_out, piece

    both, head = P("seq", "head"), P("head")
    cached = P("seq", "head", None, None)
    return jax.shard_map(
        on_device,
        mesh=mesh,
        in_specs=(
            both,
            both,
            both,
            both,
            head,
            head,
            cached,
            P(),
            P(),
            P(),
            both,
            both,
            both,
            both,
            both,
            head,
            P("head", "seq"),
        ),
        out_specs=(both, cached, P("head", "seq"), P("head", "seq")),
        check_vma=False,
    )
```

```python
import functools

import jax
import jax.numpy as jnp
from jax import lax
from jax.experimental import pallas as pl
from jax.experimental.pallas import tpu as pltpu
from jax.sharding import PartitionSpec as P

HEADS = 16
HEAD_DIM = 64
WIDTH = HEADS * HEAD_DIM
STATE = 128
BLOCK = 256
DRAFT = 8
HALF = WIDTH // 2
PACK_ROWS = 32
ROWS2 = 2 * DRAFT
HALF_HEADS = HEADS // 2
EPSILON = 1e-05
CORES = 2
VMEM_LIMIT = 40 << 20

bf16, f32 = jnp.bfloat16, jnp.float32
NN = (((1,), (0,)), ((), ()))
NT = (((1,), (1,)), ((), ()))
TN = (((0,), (0,)), ((), ()))


def dot(a, b, dims=NN):
    return lax.dot_general(a, b, dims, preferred_element_type=f32)


def parts(value, count):
    out = []
    for _ in range(count):
        piece = value.astype(bf16)
        out.append(piece)
        value = value - piece.astype(f32)
    return out


def iota(shape, axis):
    return lax.broadcasted_iota(jnp.int32, shape, axis)


def head_lanes():
    shape = (HEADS, WIDTH)
    lane_head = lax.shift_right_logical(iota(shape, 1), 6)
    return jnp.where(lane_head == iota(shape, 0), 1.0, 0.0).astype(bf16)


def spread(value, lanes):
    high, low = parts(value, 2)
    return dot(high, lanes) + dot(low, lanes)


def draft_running(vstep, rate):
    vlog = -(vstep * rate)
    row = iota(vlog.shape, 0)
    total = jnp.zeros_like(vlog)
    for j in range(DRAFT):
        total = total + jnp.where(row >= j, vlog[j : j + 1, :], 0.0)
    return vlog, total


def draft_direct(vin, vread, vwrite, vstep, rate, skip_x, lanes):
    _, vrun = draft_running(vstep, rate)
    scores = dot(vread, vwrite, NT)
    row = iota(vrun.shape, 0)
    pieces = []
    for j in range(DRAFT):
        gap = jnp.where(row >= j, vrun - vrun[j : j + 1, :], -jnp.inf)
        pieces.append(jnp.exp(gap) * vstep[j : j + 1, :] * scores[:, j : j + 1])
    pieces.append(jnp.exp(vrun))
    wide = spread(jnp.concatenate(pieces, axis=0), lanes)
    total = skip_x * vin
    for j in range(DRAFT):
        total = total + wide[j * DRAFT : (j + 1) * DRAFT, :] * vin[j : j + 1, :]
    return total, wide[DRAFT * DRAFT :, :]


def normed(y, vgate, gain):
    gated = y * (vgate / (1.0 + jnp.exp(-vgate)))
    mean = jnp.mean(gated * gated, axis=1, keepdims=True)
    return gated * lax.rsqrt(mean + EPSILON) * gain


IN_NAMES = 17


def mixer_kernel(nz, ny, nh, *refs):
    hbm, outs, vmem, scratch = (
        refs[:IN_NAMES],
        refs[IN_NAMES : IN_NAMES + 4],
        refs[IN_NAMES + 4 : 2 * IN_NAMES + 4],
        refs[2 * IN_NAMES + 4 :],
    )
    (
        x_ref,
        step_ref,
        w_ref,
        r_ref,
        rate_ref,
        skip_ref,
        res_ref,
        owner_ref,
        ids_ref,
        len_ref,
        di_ref,
        dg_ref,
        dw_ref,
        dr_ref,
        ds_ref,
        gain_ref,
        ow_ref,
    ) = vmem
    out_ref, ns_ref, vo_ref, ps_ref = outs
    (
        intra,
        decay_sq,
        lgp_send,
        lgp_recv,
        lgy,
        lgz,
        ls,
        ls_in,
        st_send,
        st_recv,
        en_send,
        en_recv,
        ent,
        ent_out,
        fin,
        fin32,
        pk,
        pk_pair,
        pky,
        pkz,
        pkf,
        pkf_other,
        own_a,
        own_b,
        ya,
        zb,
        ga,
        gb,
        ga_other,
        gb_other,
        part,
        total_ref,
        rs_send,
        rs_recv,
        fx_send,
        fx_recv,
        isem,
        sem,
        ysem,
        lsem,
        gsem,
        hsem,
    ) = scratch
    chips = nz * ny
    n = chips * CORES
    tile = HALF // chips
    me = lax.axis_index("seq")
    mh = lax.axis_index("head")
    core = lax.rem(me, CORES)
    chip = me // CORES
    my_y = lax.rem(chip, ny)
    my_z = chip // ny
    pair = me + 1 - 2 * core
    is_low = core == 0

    def y_peer(k):
        return (my_z * ny + lax.rem(my_y + k, ny)) * CORES + core

    def z_at(k):
        return lax.rem(my_z + k + nz, nz)

    def z_peer(k):
        return (z_at(k) * ny + my_y) * CORES + core

    def push(src, dst, send, recv, peer, axis="seq"):
        pltpu.make_async_remote_copy(
            src_ref=src,
            dst_ref=dst,
            send_sem=send,
            recv_sem=recv,
            device_id={axis: peer},
            device_id_type=pl.DeviceIdType.MESH,
        ).start()

    def drain(ref, which):
        pltpu.make_async_copy(ref, ref, which).wait()

    for k in range(IN_NAMES):
        pltpu.make_async_copy(hbm[k], vmem[k], isem.at[k]).start()

    def load(*which):
        for k in which:
            pltpu.make_async_copy(hbm[k], vmem[k], isem.at[k]).wait()

    barrier = pltpu.get_barrier_semaphore()

    def greet(axis, peer):
        pl.semaphore_signal(
            barrier,
            inc=1,
            device_id={axis: peer},
            device_id_type=pl.DeviceIdType.MESH,
        )

    def greet_chip(k, _):
        greet("seq", lax.rem(chip + k, chips) * CORES + core)
        return 0

    def greet_head(k, _):
        greet("head", lax.rem(mh + k, nh))
        return 0

    greet("seq", pair)
    lax.fori_loop(1, chips, greet_chip, 0)
    lax.fori_loop(1, nh, greet_head, 0)

    lanes = head_lanes()
    square = (BLOCK, BLOCK)
    causal = iota(square, 0) >= iota(square, 1)
    tri = jnp.where(causal, 1.0, 0.0).astype(bf16)
    load(1, 4)
    rate = rate_ref[...]
    step_t = jnp.concatenate([step_ref[...], jnp.zeros((STATE - HEADS, BLOCK), f32)], axis=0)
    step = jnp.transpose(step_t)[:, 0:HEADS]
    logd = -(step * rate)
    running = sum(dot(tri, piece) for piece in reversed(parts(logd, 3)))
    last = running[BLOCK - 1 : BLOCK, :]
    lgp_send[...] = jnp.zeros((1, STATE), f32)
    lgp_send[:, 0:HEADS] = last
    to_end = jnp.exp(last - running) * step

    pl.semaphore_wait(barrier, chips + nh - 1)
    push(lgp_send, lgp_recv, sem.at[0], sem.at[1], pair)

    load(0, 2)
    weighted = (x_ref[...].astype(f32) * spread(to_end, lanes)).astype(bf16)
    ls[...] = dot(weighted, w_ref[...], TN)
    own_half = pl.ds(pl.multiple_of(core * HALF, HALF), HALF)
    pair_half = pl.ds(pl.multiple_of((1 - core) * HALF, HALF), HALF)
    push(ls.at[pair_half], ls_in, sem.at[2], sem.at[3], pair)

    load(5, 6, 7, 8, 9, 10, 11, 12, 13, 14, 15)
    owner = owner_ref[...]
    mine = owner == me
    mine_wide = jnp.broadcast_to(jnp.where(mine, 1.0, 0.0), (DRAFT, n))
    chosen = jnp.sum(mine_wide * ids_ref[...].astype(f32), axis=1, keepdims=True)
    candidates = di_ref.shape[0]
    pick = jnp.where(
        iota((DRAFT, candidates), 1) == chosen.astype(jnp.int32), 1.0, 0.0
    ).astype(bf16)
    vin = dot(pick, di_ref[...])
    vgate = dot(pick, dg_ref[...])
    vwrite = dot(pick, dw_ref[...])
    vread = dot(pick, dr_ref[...])
    vstep = sum(dot(pick, piece) for piece in reversed(parts(ds_ref[...], 3)))
    skip_x = spread(jnp.broadcast_to(skip_ref[...], (DRAFT, HEADS)), lanes)
    gain = gain_ref[...]
    direct, reach_x = draft_direct(
        vin, vread.astype(bf16), vwrite.astype(bf16), vstep, rate, skip_x, lanes
    )
    inter = dot(vread.astype(bf16), res_ref[...], NT)
    hidden = normed(direct + reach_x * inter, vgate, gain).astype(bf16)
    own_a[...] = hidden[:, :HALF]
    own_b[...] = hidden[:, HALF:]
    ya[my_y] = own_a[...]
    zb[my_z] = own_b[...]
    for k in range(1, ny):
        push(own_a, ya.at[my_y], gsem.at[0, k], gsem.at[1, k], y_peer(k))
    for k in range(1, nz):
        push(own_b, zb.at[my_z], gsem.at[2, k], gsem.at[3, k], z_peer(k))

    first = jnp.where(owner[:, 0:1] == me, 1.0, 0.0)
    step_high, step_low = parts(vstep, 2)
    blank = jnp.zeros((DRAFT, STATE - HEADS), f32)
    small = jnp.concatenate(
        [
            vread,
            vwrite,
            step_high.astype(f32),
            blank,
            step_low.astype(f32),
            blank,
            jnp.zeros((DRAFT, HALF), f32),
        ],
        axis=1,
    )
    pk[...] = (
        jnp.concatenate([vin, vgate, small, jnp.zeros((DRAFT, WIDTH), f32)], axis=0) * first
    ).astype(bf16)
    push(pk, pk_pair, sem.at[6], sem.at[7], pair)

    drain(lgp_send, sem.at[0])
    drain(lgp_recv, sem.at[1])
    own_log, other_log = lgp_send[...], lgp_recv[...]
    log_0 = jnp.where(is_low, own_log, other_log)
    log_1 = jnp.where(is_low, other_log, own_log)
    lgy[my_y] = own_log + other_log
    for k in range(1, ny):
        push(lgy.at[my_y], lgy.at[my_y], lsem.at[0, k], lsem.at[1, k], y_peer(k))

    head_eye = iota((HEADS, STATE), 0) == iota((HEADS, STATE), 1)

    def head_rows(row):
        wide = jnp.where(head_eye, jnp.broadcast_to(row, (HEADS, STATE)), 0.0)
        return jnp.broadcast_to(jnp.sum(wide, axis=1, keepdims=True), (HEADS, STATE))

    def half_rows(row):
        wide = jnp.exp(head_rows(row))
        return jnp.where(is_low, wide[0:HALF_HEADS, :], wide[HALF_HEADS:, :])

    decay_0, decay_1 = half_rows(log_0), half_rows(log_1)
    drain(ls_in, sem.at[2])
    drain(ls_in, sem.at[3])
    own_rows, other_rows = ls[own_half, :], ls_in[...]
    state_0 = jnp.where(is_low, own_rows, other_rows)
    state_1 = jnp.where(is_low, other_rows, own_rows)
    ls_in[...] = state_0
    chip_state = jnp.concatenate(
        [
            state_0[h * HEAD_DIM : (h + 1) * HEAD_DIM, :] * decay_1[h : h + 1, :]
            + state_1[h * HEAD_DIM : (h + 1) * HEAD_DIM, :]
            for h in range(HALF_HEADS)
        ],
        axis=0,
    )
    st_send[...] = chip_state.astype(bf16).reshape(chips, tile, STATE)

    def send_states(k, _):
        to = lax.rem(chip + k, chips)
        push(st_send.at[to], st_recv.at[chip], sem.at[8], sem.at[9], to * CORES + core)
        return 0

    lax.fori_loop(1, chips, send_states, 0)
    st_recv[chip] = st_send[chip]

    drain(pk, sem.at[6])
    drain(pk_pair, sem.at[7])
    chip_pack = (pk[...].astype(f32) + pk_pair[...].astype(f32)).astype(bf16)
    pky[my_y] = jnp.where(is_low, chip_pack[:, :HALF], chip_pack[:, HALF:])
    for k in range(1, ny):
        push(pky.at[my_y], pky.at[my_y], ysem.at[0, k], ysem.at[1, k], y_peer(k))

    for k in range(1, ny):
        drain(lgy.at[0], lsem.at[0, k])
        drain(lgy.at[0], lsem.at[1, k])
    lgz[my_z] = lgy[...]
    for k in range(1, nz):
        push(lgy, lgz.at[my_z], lsem.at[2, k], lsem.at[3, k], z_peer(k))

    vlog, vrun = draft_running(vstep, rate)
    kept = jnp.sum(jnp.where(mine, len_ref[...], 0).astype(f32), axis=1, keepdims=True)
    live = iota(vlog.shape, 0).astype(f32) < kept
    reach = jnp.sum(jnp.where(live, vlog, 0.0), axis=0, keepdims=True)
    tail = jnp.exp(jnp.where(live, reach - vrun, -jnp.inf)) * vstep
    rows_keep = vin * spread(tail, lanes)
    high, low = parts(rows_keep, 2)
    twice = jnp.concatenate([high.astype(f32), low.astype(f32)], axis=0).astype(bf16)
    write_twice = jnp.concatenate([vwrite, vwrite], axis=0).astype(bf16)
    reach_rows = head_rows(
        jnp.concatenate([jnp.exp(reach), jnp.zeros((1, STATE - HEADS), f32)], axis=1)
    )

    for k in range(1, ny):
        drain(own_a, gsem.at[0, k])
        drain(own_a, gsem.at[1, k])
    for k in range(1, nz):
        drain(own_b, gsem.at[2, k])
        drain(own_b, gsem.at[3, k])
    ga[my_z] = ya[...]
    gb[my_y] = zb[...]
    for k in range(1, nz):
        push(ya, ga.at[my_z], gsem.at[4, k], gsem.at[5, k], z_peer(k))
    for k in range(1, ny):
        push(zb, gb.at[my_y], gsem.at[6, k], gsem.at[7, k], y_peer(k))

    for k in range(1, ny):
        drain(pky.at[0], ysem.at[0, k])
        drain(pky.at[0], ysem.at[1, k])
    pkf[...] = jnp.sum(pky[...].astype(f32), axis=0).astype(bf16)
    pkz[my_z] = pkf[...]
    for k in range(1, nz):
        push(pkf, pkz.at[my_z], lsem.at[4, k], lsem.at[5, k], z_peer(k))

    for k in range(1, nz):
        drain(lgy, lsem.at[2, k])
        drain(lgy, lsem.at[3, k])
    logs = lgz[...].reshape(chips, STATE)
    tile_head = core * HALF_HEADS + (chip * tile) // HEAD_DIM
    column = jnp.sum(
        jnp.where(iota((chips, STATE), 1) == tile_head, logs, 0.0), axis=1, keepdims=True
    )
    decay_sq[...] = jnp.broadcast_to(jnp.exp(column), (chips, STATE))
    drain(st_recv.at[pl.ds(0, chips - 1)], sem.at[9])
    drain(st_send.at[pl.ds(0, chips - 1)], sem.at[8])

    def scan_block(j, state):
        en_send[j, 0] = state.astype(bf16)
        return state * decay_sq[pl.ds(j, 1), :] + st_recv[j].astype(f32)

    final = lax.fori_loop(0, chips, scan_block, jnp.zeros((tile, STATE), f32)).astype(bf16)
    en_send[:, 1] = jnp.broadcast_to(final[None], (chips, tile, STATE))

    def send_entering(k, _):
        to = lax.rem(chip + k, chips)
        push(en_send.at[to], en_recv.at[chip], sem.at[10], sem.at[11], to * CORES + core)
        return 0

    lax.fori_loop(1, chips, send_entering, 0)
    en_recv[chip] = en_send[chip]

    load(3)
    scores = jnp.where(causal, dot(r_ref[...], w_ref[...], NT), 0.0)
    lanes128 = iota((BLOCK, STATE), 1)
    wide_run = jnp.concatenate([running, jnp.zeros((BLOCK, STATE - HEADS), f32)], axis=1)
    run_t = jnp.transpose(wide_run)

    for two in range(HALF_HEADS):
        columns = pl.ds(two * STATE, STATE)
        pair_x = x_ref[:, columns]
        sides = []
        for h in (2 * two, 2 * two + 1):
            gap = running[:, h : h + 1] - run_t[h : h + 1, :]
            decayed = jnp.exp(jnp.where(causal, gap, -jnp.inf))
            mixing = (scores * decayed * step_t[h : h + 1, :]).astype(bf16)
            sides.append(dot(mixing, pair_x))
        intra[:, columns] = jnp.where(lanes128 < HEAD_DIM, sides[0], sides[1])
    exp_x = spread(jnp.exp(running), lanes)

    drain(en_recv.at[pl.ds(0, chips - 1)], sem.at[11])
    drain(en_send.at[pl.ds(0, chips - 1)], sem.at[10])
    fin[own_half, :] = en_recv[:, 1].reshape(HALF, STATE)
    push(fin.at[own_half], fin.at[own_half], sem.at[12], sem.at[13], pair)
    enter_0 = en_recv[:, 0].reshape(HALF, STATE)
    enter_1 = jnp.concatenate(
        [
            enter_0[h * HEAD_DIM : (h + 1) * HEAD_DIM, :].astype(f32) * decay_0[h : h + 1, :]
            + ls_in[h * HEAD_DIM : (h + 1) * HEAD_DIM, :]
            for h in range(HALF_HEADS)
        ],
        axis=0,
    ).astype(bf16)
    ent_out[...] = jnp.where(is_low, enter_1, enter_0)
    push(ent_out, ent.at[own_half], sem.at[14], sem.at[15], pair)
    ent[own_half, :] = jnp.where(is_low, enter_0, enter_1)

    for k in range(1, nz):
        drain(ya, gsem.at[4, k])
        drain(ya, gsem.at[5, k])
    push(ga, ga_other, sem.at[16], sem.at[17], pair)
    for k in range(1, ny):
        drain(zb, gsem.at[6, k])
        drain(zb, gsem.at[7, k])
    push(gb, gb_other, sem.at[18], sem.at[19], pair)
    for k in range(1, nz):
        drain(pkf, lsem.at[4, k])
        drain(pkf, lsem.at[5, k])
    pack_mine = jnp.sum(pkz[...].astype(f32), axis=0).astype(bf16)
    pkf[...] = pack_mine
    push(pkf, pkf_other, sem.at[20], sem.at[21], pair)

    load(16)
    rows = n * DRAFT
    weight_a, weight_b = ow_ref[0:HALF, :], ow_ref[HALF:, :]

    def share(part_a, part_b):
        from_a = dot(part_a[...].reshape(rows // 2, HALF), weight_a)
        from_b = dot(part_b[...].reshape(rows // 2, HALF), weight_b)
        from_b = from_b.reshape(ny, nz, DRAFT, STATE)
        from_b = jnp.stack([from_b[k] for k in range(ny)], axis=1)
        return from_a.reshape(nz, ny, DRAFT, STATE) + from_b

    part[:, :, core] = share(ga, gb)
    drain(ga, sem.at[16])
    drain(ga, sem.at[17])
    drain(gb, sem.at[18])
    drain(gb, sem.at[19])
    part[:, :, 1 - core] = share(ga_other, gb_other)
    block_rows = rows // nh
    full = part[...].reshape(nh, block_rows, STATE)
    total_ref[...] = full
    rs_send[...] = full.astype(bf16)
    for k in range(1, nh):
        peer = lax.rem(mh + k, nh)
        push(rs_send.at[peer], rs_recv.at[mh], hsem.at[0, k], hsem.at[1, k], peer, "head")
    rs_recv[mh] = jnp.zeros((block_rows, STATE), bf16)

    drain(pkf, sem.at[20])
    drain(pkf, sem.at[21])
    pack_mine = pack_mine.astype(f32)
    pack_other = pkf_other[...].astype(f32)
    pack_low = jnp.where(is_low, pack_mine, pack_other)
    pack_high = jnp.where(is_low, pack_other, pack_mine)
    pack = jnp.concatenate([pack_low[0:ROWS2, :], pack_high[0:ROWS2, :]], axis=1)
    pin, pgate = pack[0:DRAFT, :], pack[DRAFT:, :]
    small = pack_low[ROWS2 : ROWS2 + DRAFT, :]
    pread = small[:, 0:STATE].astype(bf16)
    pwrite = small[:, STATE : 2 * STATE].astype(bf16)
    pstep = (small[:, 2 * STATE : 3 * STATE] + small[:, 3 * STATE :])[:, 0:HEADS]
    pdirect, preach = draft_direct(pin, pread, pwrite, pstep, rate, skip_x, lanes)

    drain(ent_out, sem.at[12])
    drain(ent_out, sem.at[13])
    phidden = normed(pdirect + preach * dot(pread, fin[...], NT), pgate, gain).astype(bf16)
    fix = dot(phidden, ow_ref[...])
    fx_send[...] = fix
    for k in range(1, nh):
        peer = lax.rem(mh + k, nh)
        push(fx_send, fx_recv.at[mh], hsem.at[2, k], hsem.at[3, k], peer, "head")
    fx_recv[mh] = fix

    drain(ent_out, sem.at[14])
    drain(ent_out, sem.at[15])
    inter_part = dot(r_ref[...], ent[...], NT) * exp_x
    out_ref[...] = (
        intra[...] + inter_part + skip_x[0:1, :] * x_ref[...].astype(f32)
    ).astype(bf16)

    fin32[...] = fin[...].astype(f32)
    pieces = HEAD_DIM // n
    for k in range(pieces):
        rows_at = pl.ds(me * pieces + k, HEADS, stride=HEAD_DIM)
        ps_ref[:, k * STATE : (k + 1) * STATE] = fin32[rows_at, :].astype(bf16)
    added = dot(twice, write_twice, TN)
    from_prompt = jnp.broadcast_to(first, (HEAD_DIM, STATE)) > 0.5
    for h in range(HEADS):
        span = slice(h * HEAD_DIM, (h + 1) * HEAD_DIM)
        start = jnp.where(from_prompt, fin32[span, :], res_ref[span, :].astype(f32))
        ns_ref[span, :] = (start * reach_rows[h : h + 1, :] + added[span, :]).astype(bf16)

    for k in range(1, nh):
        drain(rs_send.at[0], hsem.at[0, k])
        drain(rs_send.at[0], hsem.at[1, k])
        drain(fx_send, hsem.at[2, k])
        drain(fx_send, hsem.at[3, k])
    total = total_ref[mh] + jnp.sum(rs_recv[...].astype(f32), axis=0)
    slots = block_rows // DRAFT
    fixed = jnp.concatenate([jnp.sum(fx_recv[...], axis=0)] * slots, axis=0)
    slot = mh * slots + lax.shift_right_logical(iota(total.shape, 0), 3)
    is_prompt = slot == jnp.broadcast_to(owner[:, 0:1], total.shape)
    vo_ref[...] = jnp.where(is_prompt, fixed, total).astype(bf16)


def store_kernel(*refs):
    copies = [pltpu.make_async_copy(refs[k], refs[4 + k], refs[8].at[k]) for k in range(4)]
    for copy in copies:
        copy.start()
    for copy in copies:
        copy.wait()


def solution(mesh, nz=8, ny=4):
    n, nh = mesh.shape["seq"], mesh.shape["head"]
    chips = n // CORES
    tile = HALF // chips
    rows = n * DRAFT

    def on_device(
        prefill_input,
        prefill_step,
        write_proj,
        read_proj,
        decay_rate,
        skip_gain,
        resident_state,
        owner_slot,
        draft_ids,
        accepted_len,
        draft_input,
        draft_gate,
        draft_write,
        draft_read,
        draft_step,
        norm_gain,
        out_weight,
    ):
        vmem = pl.BlockSpec(memory_space=pltpu.VMEM)
        stay = pl.BlockSpec(memory_space=pltpu.HBM)
        args = (
            prefill_input,
            prefill_step.T,
            write_proj,
            read_proj,
            decay_rate[None],
            skip_gain[None],
            resident_state.reshape(WIDTH, STATE),
            owner_slot[None],
            draft_ids.T,
            accepted_len[None],
            draft_input,
            draft_gate,
            draft_write,
            draft_read,
            draft_step,
            norm_gain[None],
            out_weight,
        )
        args = tuple(pltpu.with_memory_space_constraint(a, pltpu.HBM) for a in args)
        block_rows = rows // nh
        scratch = [pltpu.VMEM(arg.shape, arg.dtype) for arg in args] + [
            pltpu.VMEM((BLOCK, WIDTH), f32),
            pltpu.VMEM((chips, STATE), f32),
            pltpu.VMEM((1, STATE), f32),
            pltpu.VMEM((1, STATE), f32),
            pltpu.VMEM((ny, 1, STATE), f32),
            pltpu.VMEM((nz, ny, 1, STATE), f32),
            pltpu.VMEM((WIDTH, STATE), f32),
            pltpu.VMEM((HALF, STATE), f32),
            pltpu.VMEM((chips, tile, STATE), bf16),
            pltpu.VMEM((chips, tile, STATE), bf16),
            pltpu.VMEM((chips, 2, tile, STATE), bf16),
            pltpu.VMEM((chips, 2, tile, STATE), bf16),
            pltpu.VMEM((WIDTH, STATE), bf16),
            pltpu.VMEM((HALF, STATE), bf16),
            pltpu.VMEM((WIDTH, STATE), bf16),
            pltpu.VMEM((WIDTH, STATE), f32),
            pltpu.VMEM((PACK_ROWS, WIDTH), bf16),
            pltpu.VMEM((PACK_ROWS, WIDTH), bf16),
            pltpu.VMEM((ny, PACK_ROWS, HALF), bf16),
            pltpu.VMEM((nz, PACK_ROWS, HALF), bf16),
            pltpu.VMEM((PACK_ROWS, HALF), bf16),
            pltpu.VMEM((PACK_ROWS, HALF), bf16),
            pltpu.VMEM((DRAFT, HALF), bf16),
            pltpu.VMEM((DRAFT, HALF), bf16),
            pltpu.VMEM((ny, DRAFT, HALF), bf16),
            pltpu.VMEM((nz, DRAFT, HALF), bf16),
            pltpu.VMEM((nz, ny, DRAFT, HALF), bf16),
            pltpu.VMEM((ny, nz, DRAFT, HALF), bf16),
            pltpu.VMEM((nz, ny, DRAFT, HALF), bf16),
            pltpu.VMEM((ny, nz, DRAFT, HALF), bf16),
            pltpu.VMEM((nz, ny, CORES, DRAFT, STATE), f32),
            pltpu.VMEM((nh, block_rows, STATE), f32),
            pltpu.VMEM((nh, block_rows, STATE), bf16),
            pltpu.VMEM((nh, block_rows, STATE), bf16),
            pltpu.VMEM((DRAFT, STATE), f32),
            pltpu.VMEM((nh, DRAFT, STATE), f32),
            pltpu.SemaphoreType.DMA((IN_NAMES,)),
            pltpu.SemaphoreType.DMA((22,)),
            pltpu.SemaphoreType.DMA((2, ny)),
            pltpu.SemaphoreType.DMA((6, max(ny, nz))),
            pltpu.SemaphoreType.DMA((8, max(ny, nz))),
            pltpu.SemaphoreType.DMA((4, nh)),
        ]
        shapes = (
            jax.ShapeDtypeStruct((BLOCK, WIDTH), bf16),
            jax.ShapeDtypeStruct((WIDTH, STATE), bf16),
            jax.ShapeDtypeStruct((block_rows, STATE), bf16),
            jax.ShapeDtypeStruct((HEADS, HEAD_DIM * STATE // n), bf16),
        )
        results = pl.pallas_call(
            functools.partial(mixer_kernel, nz, ny, nh),
            out_shape=shapes,
            in_specs=[stay] * len(args),
            out_specs=(vmem,) * 4,
            scratch_shapes=scratch,
            compiler_params=pltpu.CompilerParams(
                collective_id=0, has_side_effects=True, vmem_limit_bytes=VMEM_LIMIT
            ),
        )(*args)
        prefill_out, new_state, verify_out, piece = pl.pallas_call(
            store_kernel,
            out_shape=shapes,
            in_specs=[stay] * 4,
            out_specs=(stay,) * 4,
            scratch_shapes=[pltpu.SemaphoreType.DMA((4,))],
            compiler_params=pltpu.CompilerParams(vmem_limit_bytes=VMEM_LIMIT),
        )(*results)
        new_state = new_state.reshape(1, HEADS, HEAD_DIM, STATE)
        return prefill_out, new_state, verify_out, piece

    both, head = P("seq", "head"), P("head")
    cached = P("seq", "head", None, None)
    return jax.shard_map(
        on_device,
        mesh=mesh,
        in_specs=(
            both,
            both,
            both,
            both,
            head,
            head,
            cached,
            P(),
            P(),
            P(),
            both,
            both,
            both,
            both,
            both,
            head,
            P("head", "seq"),
        ),
        out_specs=(both, cached, P("head", "seq"), P("head", "seq")),
        check_vma=False,
    )
```

```python
import functools

import jax
import jax.numpy as jnp
from jax import lax
from jax.experimental import pallas as pl
from jax.experimental.pallas import tpu as pltpu
from jax.sharding import PartitionSpec as P

HEADS = 16
HEAD_DIM = 64
WIDTH = HEADS * HEAD_DIM
STATE = 128
BLOCK = 256
DRAFT = 8
HALF = WIDTH // 2
PACK = 1280
PACK_HALF = PACK // 2
ROWS2 = 2 * DRAFT
HALF_HEADS = HEADS // 2
EPSILON = 1e-05
CORES = 2
EXTRA = 8
VMEM_LIMIT = 40 << 20

bf16, f32 = jnp.bfloat16, jnp.float32
NN = (((1,), (0,)), ((), ()))
NT = (((1,), (1,)), ((), ()))
TN = (((0,), (0,)), ((), ()))


def dot(a, b, dims=NN):
    return lax.dot_general(a, b, dims, preferred_element_type=f32)


def parts(value, count):
    out = []
    for _ in range(count):
        piece = value.astype(bf16)
        out.append(piece)
        value = value - piece.astype(f32)
    return out


def iota(shape, axis):
    return lax.broadcasted_iota(jnp.int32, shape, axis)


def head_lanes():
    shape = (HEADS, WIDTH)
    lane_head = lax.shift_right_logical(iota(shape, 1), 6)
    return jnp.where(lane_head == iota(shape, 0), 1.0, 0.0).astype(bf16)


def spread(value, lanes):
    high, low = parts(value, 2)
    return dot(high, lanes) + dot(low, lanes)


def draft_running(vstep, rate):
    vlog = -(vstep * rate)
    row = iota(vlog.shape, 0)
    total = jnp.zeros_like(vlog)
    for j in range(DRAFT):
        total = total + jnp.where(row >= j, vlog[j : j + 1, :], 0.0)
    return vlog, total


def draft_direct(vin, vread, vwrite, vstep, rate, skip_x, lanes):
    _, vrun = draft_running(vstep, rate)
    scores = dot(vread, vwrite, NT)
    row = iota(vrun.shape, 0)
    pieces = []
    for j in range(DRAFT):
        gap = jnp.where(row >= j, vrun - vrun[j : j + 1, :], -jnp.inf)
        pieces.append(jnp.exp(gap) * vstep[j : j + 1, :] * scores[:, j : j + 1])
    pieces.append(jnp.exp(vrun))
    wide = spread(jnp.concatenate(pieces, axis=0), lanes)
    total = skip_x * vin
    for j in range(DRAFT):
        total = total + wide[j * DRAFT : (j + 1) * DRAFT, :] * vin[j : j + 1, :]
    return total, wide[DRAFT * DRAFT :, :]


def normed(y, vgate, gain):
    gated = y * (vgate / (1.0 + jnp.exp(-vgate)))
    mean = jnp.mean(gated * gated, axis=1, keepdims=True)
    return gated * lax.rsqrt(mean + EPSILON) * gain


IN_NAMES = 17


def mixer_kernel(nz, ny, nh, *refs):
    hbm, outs, vmem, scratch = (
        refs[:IN_NAMES],
        refs[IN_NAMES : IN_NAMES + 4],
        refs[IN_NAMES + 4 : 2 * IN_NAMES + 4],
        refs[2 * IN_NAMES + 4 :],
    )
    (
        x_ref,
        step_ref,
        w_ref,
        r_ref,
        rate_ref,
        skip_ref,
        res_ref,
        owner_ref,
        ids_ref,
        len_ref,
        di_ref,
        dg_ref,
        dw_ref,
        dr_ref,
        ds_ref,
        gain_ref,
        ow_ref,
    ) = vmem
    out_ref, ns_ref, vo_ref, ps_ref = outs
    (
        intra,
        decay_sq,
        lgp_send,
        lgp_recv,
        ls,
        ls_in,
        st_send,
        st_recv,
        en_send,
        en_recv,
        ent,
        ent_out,
        fin,
        fin32,
        pk,
        pk_pair,
        pky,
        pkz,
        pkf,
        pkf_own,
        pkf_other,
        own_a,
        own_b,
        ya,
        zb,
        ga,
        gb,
        ga_other,
        gb_other,
        part,
        total_ref,
        rs_send,
        rs_recv,
        fx_send,
        fx_recv,
        isem,
        sem,
        ysem,
        lsem,
        gsem,
        hsem,
    ) = scratch
    chips = nz * ny
    n = chips * CORES
    tile = HALF // chips
    me = lax.axis_index("seq")
    mh = lax.axis_index("head")
    core = lax.rem(me, CORES)
    chip = me // CORES
    my_y = lax.rem(chip, ny)
    my_z = chip // ny
    pair = me + 1 - 2 * core
    is_low = core == 0

    def y_peer(k):
        return (my_z * ny + lax.rem(my_y + k, ny)) * CORES + core

    def z_at(k):
        return lax.rem(my_z + k + nz, nz)

    def z_peer(k):
        return (z_at(k) * ny + my_y) * CORES + core

    def push(src, dst, send, recv, peer, axis="seq"):
        pltpu.make_async_remote_copy(
            src_ref=src,
            dst_ref=dst,
            send_sem=send,
            recv_sem=recv,
            device_id={axis: peer},
            device_id_type=pl.DeviceIdType.MESH,
        ).start()

    def drain(ref, which):
        pltpu.make_async_copy(ref, ref, which).wait()

    sent = []

    for k in range(IN_NAMES):
        pltpu.make_async_copy(hbm[k], vmem[k], isem.at[k]).start()

    def load(*which):
        for k in which:
            pltpu.make_async_copy(hbm[k], vmem[k], isem.at[k]).wait()

    barrier = pltpu.get_barrier_semaphore()

    def greet(axis, peer):
        pl.semaphore_signal(
            barrier,
            inc=1,
            device_id={axis: peer},
            device_id_type=pl.DeviceIdType.MESH,
        )

    def greet_chip(k, _):
        greet("seq", lax.rem(chip + k, chips) * CORES + core)
        return 0

    def greet_head(k, _):
        greet("head", lax.rem(mh + k, nh))
        return 0

    greet("seq", pair)
    lax.fori_loop(1, chips, greet_chip, 0)
    lax.fori_loop(1, nh, greet_head, 0)

    lanes = head_lanes()
    square = (BLOCK, BLOCK)
    causal = iota(square, 0) >= iota(square, 1)
    tri = jnp.where(causal, 1.0, 0.0).astype(bf16)
    load(1, 4)
    rate = rate_ref[...]
    step_t = jnp.concatenate([step_ref[...], jnp.zeros((STATE - HEADS, BLOCK), f32)], axis=0)
    step = jnp.transpose(step_t)[:, 0:HEADS]
    logd = -(step * rate)
    running = sum(dot(tri, piece) for piece in reversed(parts(logd, 3)))
    last = running[BLOCK - 1 : BLOCK, :]
    lgp_send[...] = jnp.zeros((1, STATE), f32)
    lgp_send[:, 0:HEADS] = last
    to_end = jnp.exp(last - running) * step

    pl.semaphore_wait(barrier, chips + nh - 1)
    push(lgp_send, lgp_recv, sem.at[0], sem.at[1], pair)

    load(0, 2)
    weighted = (x_ref[...].astype(f32) * spread(to_end, lanes)).astype(bf16)
    ls[...] = dot(weighted, w_ref[...], TN)
    own_half = pl.ds(pl.multiple_of(core * HALF, HALF), HALF)
    pair_half = pl.ds(pl.multiple_of((1 - core) * HALF, HALF), HALF)
    push(ls.at[pair_half], ls_in, sem.at[2], sem.at[3], pair)

    load(5, 6, 7, 8, 9, 10, 11, 12, 13, 14, 15)
    owner = owner_ref[...]
    mine = owner == me
    mine_wide = jnp.broadcast_to(jnp.where(mine, 1.0, 0.0), (DRAFT, n))
    chosen = jnp.sum(mine_wide * ids_ref[...].astype(f32), axis=1, keepdims=True)
    candidates = di_ref.shape[0]
    pick = jnp.where(
        iota((DRAFT, candidates), 1) == chosen.astype(jnp.int32), 1.0, 0.0
    ).astype(bf16)
    vin = dot(pick, di_ref[...])
    vgate = dot(pick, dg_ref[...])
    vwrite = dot(pick, dw_ref[...])
    vread = dot(pick, dr_ref[...])
    vstep = sum(dot(pick, piece) for piece in reversed(parts(ds_ref[...], 3)))
    skip_x = spread(jnp.broadcast_to(skip_ref[...], (DRAFT, HEADS)), lanes)
    gain = gain_ref[...]
    direct, reach_x = draft_direct(
        vin, vread.astype(bf16), vwrite.astype(bf16), vstep, rate, skip_x, lanes
    )
    inter = dot(vread.astype(bf16), res_ref[...], NT)
    hidden = normed(direct + reach_x * inter, vgate, gain).astype(bf16)
    own_a[...] = hidden[:, :HALF]
    own_b[...] = hidden[:, HALF:]
    ya[my_y] = own_a[...]
    zb[my_z] = own_b[...]
    for k in range(1, ny):
        push(own_a, ya.at[my_y], gsem.at[0, k], gsem.at[0, 0], y_peer(k))
        sent.append((own_a, gsem.at[0, k]))
    for k in range(1, nz):
        push(own_b, zb.at[my_z], gsem.at[1, k], gsem.at[1, 0], z_peer(k))
        sent.append((own_b, gsem.at[1, k]))

    first = jnp.where(owner[:, 0:1] == me, 1.0, 0.0)
    step_high, step_low = parts(vstep, 2)
    blank = jnp.zeros((DRAFT, STATE - HEADS), f32)
    pk[...] = (
        jnp.concatenate(
            [
                jnp.concatenate([vin, vread, step_high.astype(f32), blank], axis=1),
                jnp.concatenate([vgate, vwrite, step_low.astype(f32), blank], axis=1),
            ],
            axis=0,
        )
        * first
    ).astype(bf16)
    push(pk, pk_pair, sem.at[6], sem.at[7], pair)

    sent.append((lgp_send, sem.at[0]))
    drain(lgp_recv, sem.at[1])
    own_log, other_log = lgp_send[...], lgp_recv[...]
    log_0 = jnp.where(is_low, own_log, other_log)
    log_1 = jnp.where(is_low, other_log, own_log)

    head_eye = iota((HEADS, STATE), 0) == iota((HEADS, STATE), 1)

    def head_rows(row):
        wide = jnp.where(head_eye, jnp.broadcast_to(row, (HEADS, STATE)), 0.0)
        return jnp.broadcast_to(jnp.sum(wide, axis=1, keepdims=True), (HEADS, STATE))

    def half_rows(row):
        wide = head_rows(row)
        return jnp.where(is_low, wide[0:HALF_HEADS, :], wide[HALF_HEADS:, :])

    decay_0, decay_1 = jnp.exp(half_rows(log_0)), jnp.exp(half_rows(log_1))
    chip_log = half_rows(own_log + other_log)
    log_rows = jnp.stack([piece.astype(f32) for piece in parts(chip_log, 3)], axis=1)
    log_rows = jnp.concatenate(
        [log_rows, jnp.zeros((HALF_HEADS, EXTRA - 3, STATE), f32)], axis=1
    )
    sharing = HEAD_DIM // tile
    log_rows = jnp.broadcast_to(log_rows[:, None], (HALF_HEADS, sharing, EXTRA, STATE))
    st_send[:, tile:, :] = log_rows.reshape(chips, EXTRA, STATE).astype(bf16)
    sent.append((ls_in, sem.at[2]))
    drain(ls_in, sem.at[3])
    own_rows, other_rows = ls[own_half, :], ls_in[...]
    state_0 = jnp.where(is_low, own_rows, other_rows)
    state_1 = jnp.where(is_low, other_rows, own_rows)
    ls_in[...] = state_0
    chip_state = jnp.concatenate(
        [
            state_0[h * HEAD_DIM : (h + 1) * HEAD_DIM, :] * decay_1[h : h + 1, :]
            + state_1[h * HEAD_DIM : (h + 1) * HEAD_DIM, :]
            for h in range(HALF_HEADS)
        ],
        axis=0,
    )
    st_send[:, 0:tile, :] = chip_state.astype(bf16).reshape(chips, tile, STATE)

    def send_states(k, _):
        to = lax.rem(chip + k, chips)
        push(st_send.at[to], st_recv.at[chip], sem.at[8], sem.at[9], to * CORES + core)
        return 0

    lax.fori_loop(1, chips, send_states, 0)
    st_recv[chip] = st_send[chip]

    sent.append((pk, sem.at[6]))
    drain(pk_pair, sem.at[7])
    chip_pack = (pk[...].astype(f32) + pk_pair[...].astype(f32)).astype(bf16)
    pky[my_y] = jnp.where(is_low, chip_pack[:, :PACK_HALF], chip_pack[:, PACK_HALF:])
    for k in range(1, ny):
        push(pky.at[my_y], pky.at[my_y], ysem.at[k], ysem.at[0], y_peer(k))
        sent.append((pky.at[my_y], ysem.at[k]))

    vlog, vrun = draft_running(vstep, rate)
    kept = jnp.sum(jnp.where(mine, len_ref[...], 0).astype(f32), axis=1, keepdims=True)
    live = iota(vlog.shape, 0).astype(f32) < kept
    reach = jnp.sum(jnp.where(live, vlog, 0.0), axis=0, keepdims=True)
    tail = jnp.exp(jnp.where(live, reach - vrun, -jnp.inf)) * vstep
    rows_keep = vin * spread(tail, lanes)
    high, low = parts(rows_keep, 2)
    twice = jnp.concatenate([high.astype(f32), low.astype(f32)], axis=0).astype(bf16)
    write_twice = jnp.concatenate([vwrite, vwrite], axis=0).astype(bf16)
    reach_rows = head_rows(
        jnp.concatenate([jnp.exp(reach), jnp.zeros((1, STATE - HEADS), f32)], axis=1)
    )

    drain(ya.at[pl.ds(0, ny - 1)], gsem.at[0, 0])
    drain(zb.at[pl.ds(0, nz - 1)], gsem.at[1, 0])
    ga[my_z] = ya[...]
    gb[my_y] = zb[...]
    for k in range(1, nz):
        push(ya, ga.at[my_z], gsem.at[2, k], gsem.at[2, 0], z_peer(k))
        sent.append((ya, gsem.at[2, k]))
    for k in range(1, ny):
        push(zb, gb.at[my_y], gsem.at[3, k], gsem.at[3, 0], y_peer(k))
        sent.append((zb, gsem.at[3, k]))

    drain(pky.at[pl.ds(0, ny - 1)], ysem.at[0])
    pkf[...] = jnp.sum(pky[...].astype(f32), axis=0).astype(bf16)
    pkz[my_z] = pkf[...]
    for k in range(1, nz):
        push(pkf, pkz.at[my_z], lsem.at[k], lsem.at[0], z_peer(k))
        sent.append((pkf, lsem.at[k]))

    drain(st_recv.at[pl.ds(0, chips - 1)], sem.at[9])
    sent.append((st_send.at[pl.ds(0, chips - 1)], sem.at[8]))
    logs = jnp.sum(st_recv[:, tile:, :].astype(f32), axis=1)
    decay_sq[...] = jnp.exp(logs)

    def scan_block(j, state):
        en_send[j, 0] = state.astype(bf16)
        return state * decay_sq[pl.ds(j, 1), :] + st_recv[j, 0:tile, :].astype(f32)

    final = lax.fori_loop(0, chips, scan_block, jnp.zeros((tile, STATE), f32)).astype(bf16)
    en_send[:, 1] = jnp.broadcast_to(final[None], (chips, tile, STATE))

    def send_entering(k, _):
        to = lax.rem(chip + k, chips)
        push(en_send.at[to], en_recv.at[chip], sem.at[10], sem.at[11], to * CORES + core)
        return 0

    lax.fori_loop(1, chips, send_entering, 0)
    en_recv[chip] = en_send[chip]

    load(3)
    scores = jnp.where(causal, dot(r_ref[...], w_ref[...], NT), 0.0)
    lanes128 = iota((BLOCK, STATE), 1)
    wide_run = jnp.concatenate([running, jnp.zeros((BLOCK, STATE - HEADS), f32)], axis=1)
    run_t = jnp.transpose(wide_run)

    for two in range(HALF_HEADS):
        columns = pl.ds(two * STATE, STATE)
        pair_x = x_ref[:, columns]
        sides = []
        for h in (2 * two, 2 * two + 1):
            gap = running[:, h : h + 1] - run_t[h : h + 1, :]
            decayed = jnp.exp(jnp.where(causal, gap, -jnp.inf))
            mixing = (scores * decayed * step_t[h : h + 1, :]).astype(bf16)
            sides.append(dot(mixing, pair_x))
        intra[:, columns] = jnp.where(lanes128 < HEAD_DIM, sides[0], sides[1])
    exp_x = spread(jnp.exp(running), lanes)

    drain(ga.at[pl.ds(0, nz - 1)], gsem.at[2, 0])
    push(ga, ga_other, sem.at[16], sem.at[17], pair)
    drain(gb.at[pl.ds(0, ny - 1)], gsem.at[3, 0])
    push(gb, gb_other, sem.at[18], sem.at[19], pair)
    drain(pkz.at[pl.ds(0, nz - 1)], lsem.at[0])
    pack_mine = jnp.sum(pkz[...].astype(f32), axis=0).astype(bf16)
    pkf_own[...] = pack_mine
    push(pkf_own, pkf_other, sem.at[20], sem.at[21], pair)
    sent.extend([(ga, sem.at[16]), (gb, sem.at[18]), (pkf_own, sem.at[20])])

    load(16)
    rows = n * DRAFT
    weight_a, weight_b = ow_ref[0:HALF, :], ow_ref[HALF:, :]

    def share(part_a, part_b):
        from_a = dot(part_a[...].reshape(rows // 2, HALF), weight_a)
        from_b = dot(part_b[...].reshape(rows // 2, HALF), weight_b)
        from_b = from_b.reshape(ny, nz, DRAFT, STATE)
        from_b = jnp.stack([from_b[k] for k in range(ny)], axis=1)
        return from_a.reshape(nz, ny, DRAFT, STATE) + from_b

    part[:, :, core] = share(ga, gb)

    drain(en_recv.at[pl.ds(0, chips - 1)], sem.at[11])
    sent.append((en_send.at[pl.ds(0, chips - 1)], sem.at[10]))
    fin[own_half, :] = en_recv[:, 1].reshape(HALF, STATE)
    push(fin.at[own_half], fin.at[own_half], sem.at[12], sem.at[13], pair)
    enter_0 = en_recv[:, 0].reshape(HALF, STATE)
    enter_1 = jnp.concatenate(
        [
            enter_0[h * HEAD_DIM : (h + 1) * HEAD_DIM, :].astype(f32) * decay_0[h : h + 1, :]
            + ls_in[h * HEAD_DIM : (h + 1) * HEAD_DIM, :]
            for h in range(HALF_HEADS)
        ],
        axis=0,
    ).astype(bf16)
    ent_out[...] = jnp.where(is_low, enter_1, enter_0)
    push(ent_out, ent.at[own_half], sem.at[14], sem.at[15], pair)
    ent[own_half, :] = jnp.where(is_low, enter_0, enter_1)

    drain(ga, sem.at[17])
    drain(gb, sem.at[19])
    part[:, :, 1 - core] = share(ga_other, gb_other)
    block_rows = rows // nh
    full = part[...].reshape(nh, block_rows, STATE)
    total_ref[...] = full
    rs_send[...] = full.astype(bf16)
    for k in range(1, nh):
        peer = lax.rem(mh + k, nh)
        push(rs_send.at[peer], rs_recv.at[mh], hsem.at[0, k], hsem.at[0, 0], peer, "head")
        sent.append((rs_send.at[0], hsem.at[0, k]))
    rs_recv[mh] = jnp.zeros((block_rows, STATE), bf16)

    drain(pkf_other, sem.at[21])
    pack_mine = pack_mine.astype(f32)
    pack_other = pkf_other[...].astype(f32)
    pack_low = jnp.where(is_low, pack_mine, pack_other)
    pack_high = jnp.where(is_low, pack_other, pack_mine)
    pack = jnp.concatenate([pack_low, pack_high], axis=1)
    pin, pgate = pack[0:DRAFT, 0:WIDTH], pack[DRAFT:, 0:WIDTH]
    pread = pack[0:DRAFT, WIDTH : WIDTH + STATE].astype(bf16)
    pwrite = pack[DRAFT:, WIDTH : WIDTH + STATE].astype(bf16)
    pstep = (pack[0:DRAFT, WIDTH + STATE :] + pack[DRAFT:, WIDTH + STATE :])[:, 0:HEADS]
    pdirect, preach = draft_direct(pin, pread, pwrite, pstep, rate, skip_x, lanes)

    sent.append((ent_out, sem.at[12]))
    drain(ent_out, sem.at[13])
    phidden = normed(pdirect + preach * dot(pread, fin[...], NT), pgate, gain).astype(bf16)
    fix = dot(phidden, ow_ref[...])
    fx_send[...] = fix
    for k in range(1, nh):
        peer = lax.rem(mh + k, nh)
        push(fx_send, fx_recv.at[mh], hsem.at[1, k], hsem.at[1, 0], peer, "head")
        sent.append((fx_send, hsem.at[1, k]))
    fx_recv[mh] = fix

    sent.append((ent_out, sem.at[14]))
    drain(ent_out, sem.at[15])
    inter_part = dot(r_ref[...], ent[...], NT) * exp_x
    out_ref[...] = (
        intra[...] + inter_part + skip_x[0:1, :] * x_ref[...].astype(f32)
    ).astype(bf16)

    fin32[...] = fin[...].astype(f32)
    pieces = HEAD_DIM // n
    for k in range(pieces):
        rows_at = pl.ds(me * pieces + k, HEADS, stride=HEAD_DIM)
        ps_ref[:, k * STATE : (k + 1) * STATE] = fin32[rows_at, :].astype(bf16)
    added = dot(twice, write_twice, TN)
    from_prompt = jnp.broadcast_to(first, (HEAD_DIM, STATE)) > 0.5
    for h in range(HEADS):
        span = slice(h * HEAD_DIM, (h + 1) * HEAD_DIM)
        start = jnp.where(from_prompt, fin32[span, :], res_ref[span, :].astype(f32))
        ns_ref[span, :] = (start * reach_rows[h : h + 1, :] + added[span, :]).astype(bf16)

    if nh > 1:
        drain(rs_recv.at[pl.ds(0, nh - 1)], hsem.at[0, 0])
        drain(fx_recv.at[pl.ds(0, nh - 1)], hsem.at[1, 0])
    total = total_ref[mh] + jnp.sum(rs_recv[...].astype(f32), axis=0)
    slots = block_rows // DRAFT
    fixed = jnp.concatenate([jnp.sum(fx_recv[...], axis=0)] * slots, axis=0)
    slot = mh * slots + lax.shift_right_logical(iota(total.shape, 0), 3)
    is_prompt = slot == jnp.broadcast_to(owner[:, 0:1], total.shape)
    vo_ref[...] = jnp.where(is_prompt, fixed, total).astype(bf16)
    for ref, which in sent:
        drain(ref, which)


def store_kernel(*refs):
    copies = [pltpu.make_async_copy(refs[k], refs[4 + k], refs[8].at[k]) for k in range(4)]
    for copy in copies:
        copy.start()
    for copy in copies:
        copy.wait()


def solution(mesh, nz=8, ny=4):
    n, nh = mesh.shape["seq"], mesh.shape["head"]
    chips = n // CORES
    tile = HALF // chips
    rows = n * DRAFT

    def on_device(
        prefill_input,
        prefill_step,
        write_proj,
        read_proj,
        decay_rate,
        skip_gain,
        resident_state,
        owner_slot,
        draft_ids,
        accepted_len,
        draft_input,
        draft_gate,
        draft_write,
        draft_read,
        draft_step,
        norm_gain,
        out_weight,
    ):
        vmem = pl.BlockSpec(memory_space=pltpu.VMEM)
        stay = pl.BlockSpec(memory_space=pltpu.HBM)
        args = (
            prefill_input,
            prefill_step.T,
            write_proj,
            read_proj,
            decay_rate[None],
            skip_gain[None],
            resident_state.reshape(WIDTH, STATE),
            owner_slot[None],
            draft_ids.T,
            accepted_len[None],
            draft_input,
            draft_gate,
            draft_write,
            draft_read,
            draft_step,
            norm_gain[None],
            out_weight,
        )
        args = tuple(pltpu.with_memory_space_constraint(a, pltpu.HBM) for a in args)
        block_rows = rows // nh
        scratch = [pltpu.VMEM(arg.shape, arg.dtype) for arg in args] + [
            pltpu.VMEM((BLOCK, WIDTH), f32),
            pltpu.VMEM((chips, STATE), f32),
            pltpu.VMEM((1, STATE), f32),
            pltpu.VMEM((1, STATE), f32),
            pltpu.VMEM((WIDTH, STATE), f32),
            pltpu.VMEM((HALF, STATE), f32),
            pltpu.VMEM((chips, tile + EXTRA, STATE), bf16),
            pltpu.VMEM((chips, tile + EXTRA, STATE), bf16),
            pltpu.VMEM((chips, 2, tile, STATE), bf16),
            pltpu.VMEM((chips, 2, tile, STATE), bf16),
            pltpu.VMEM((WIDTH, STATE), bf16),
            pltpu.VMEM((HALF, STATE), bf16),
            pltpu.VMEM((WIDTH, STATE), bf16),
            pltpu.VMEM((WIDTH, STATE), f32),
            pltpu.VMEM((ROWS2, PACK), bf16),
            pltpu.VMEM((ROWS2, PACK), bf16),
            pltpu.VMEM((ny, ROWS2, PACK_HALF), bf16),
            pltpu.VMEM((nz, ROWS2, PACK_HALF), bf16),
            pltpu.VMEM((ROWS2, PACK_HALF), bf16),
            pltpu.VMEM((ROWS2, PACK_HALF), bf16),
            pltpu.VMEM((ROWS2, PACK_HALF), bf16),
            pltpu.VMEM((DRAFT, HALF), bf16),
            pltpu.VMEM((DRAFT, HALF), bf16),
            pltpu.VMEM((ny, DRAFT, HALF), bf16),
            pltpu.VMEM((nz, DRAFT, HALF), bf16),
            pltpu.VMEM((nz, ny, DRAFT, HALF), bf16),
            pltpu.VMEM((ny, nz, DRAFT, HALF), bf16),
            pltpu.VMEM((nz, ny, DRAFT, HALF), bf16),
            pltpu.VMEM((ny, nz, DRAFT, HALF), bf16),
            pltpu.VMEM((nz, ny, CORES, DRAFT, STATE), f32),
            pltpu.VMEM((nh, block_rows, STATE), f32),
            pltpu.VMEM((nh, block_rows, STATE), bf16),
            pltpu.VMEM((nh, block_rows, STATE), bf16),
            pltpu.VMEM((DRAFT, STATE), f32),
            pltpu.VMEM((nh, DRAFT, STATE), f32),
            pltpu.SemaphoreType.DMA((IN_NAMES,)),
            pltpu.SemaphoreType.DMA((22,)),
            pltpu.SemaphoreType.DMA((ny,)),
            pltpu.SemaphoreType.DMA((nz,)),
            pltpu.SemaphoreType.DMA((4, max(ny, nz))),
            pltpu.SemaphoreType.DMA((2, nh)),
        ]
        shapes = (
            jax.ShapeDtypeStruct((BLOCK, WIDTH), bf16),
            jax.ShapeDtypeStruct((WIDTH, STATE), bf16),
            jax.ShapeDtypeStruct((block_rows, STATE), bf16),
            jax.ShapeDtypeStruct((HEADS, HEAD_DIM * STATE // n), bf16),
        )
        results = pl.pallas_call(
            functools.partial(mixer_kernel, nz, ny, nh),
            out_shape=shapes,
            in_specs=[stay] * len(args),
            out_specs=(vmem,) * 4,
            scratch_shapes=scratch,
            compiler_params=pltpu.CompilerParams(
                collective_id=0, has_side_effects=True, vmem_limit_bytes=VMEM_LIMIT
            ),
        )(*args)
        prefill_out, new_state, verify_out, piece = pl.pallas_call(
            store_kernel,
            out_shape=shapes,
            in_specs=[stay] * 4,
            out_specs=(stay,) * 4,
            scratch_shapes=[pltpu.SemaphoreType.DMA((4,))],
            compiler_params=pltpu.CompilerParams(vmem_limit_bytes=VMEM_LIMIT),
        )(*results)
        new_state = new_state.reshape(1, HEADS, HEAD_DIM, STATE)
        return prefill_out, new_state, verify_out, piece

    both, head = P("seq", "head"), P("head")
    cached = P("seq", "head", None, None)
    return jax.shard_map(
        on_device,
        mesh=mesh,
        in_specs=(
            both,
            both,
            both,
            both,
            head,
            head,
            cached,
            P(),
            P(),
            P(),
            both,
            both,
            both,
            both,
            both,
            head,
            P("head", "seq"),
        ),
        out_specs=(both, cached, P("head", "seq"), P("head", "seq")),
        check_vma=False,
    )
```

```python
import functools

import jax
import jax.numpy as jnp
from jax import lax
from jax.experimental import pallas as pl
from jax.experimental.pallas import tpu as pltpu
from jax.sharding import PartitionSpec as P

HEADS = 16
HEAD_DIM = 64
WIDTH = HEADS * HEAD_DIM
STATE = 128
BLOCK = 256
DRAFT = 8
HALF = WIDTH // 2
PACK = 1280
PACK_HALF = PACK // 2
ROWS2 = 2 * DRAFT
HALF_HEADS = HEADS // 2
EPSILON = 1e-05
CORES = 2
EXTRA = 8
VMEM_LIMIT = 40 << 20

bf16, f32 = jnp.bfloat16, jnp.float32
NN = (((1,), (0,)), ((), ()))
NT = (((1,), (1,)), ((), ()))
TN = (((0,), (0,)), ((), ()))


def dot(a, b, dims=NN):
    return lax.dot_general(a, b, dims, preferred_element_type=f32)


def parts(value, count):
    out = []
    for _ in range(count):
        piece = value.astype(bf16)
        out.append(piece)
        value = value - piece.astype(f32)
    return out


def iota(shape, axis):
    return lax.broadcasted_iota(jnp.int32, shape, axis)


def head_lanes():
    shape = (HEADS, WIDTH)
    lane_head = lax.shift_right_logical(iota(shape, 1), 6)
    return jnp.where(lane_head == iota(shape, 0), 1.0, 0.0).astype(bf16)


def spread(value, lanes):
    high, low = parts(value, 2)
    return dot(high, lanes) + dot(low, lanes)


def draft_running(vstep, rate):
    vlog = -(vstep * rate)
    row = iota(vlog.shape, 0)
    total = jnp.zeros_like(vlog)
    for j in range(DRAFT):
        total = total + jnp.where(row >= j, vlog[j : j + 1, :], 0.0)
    return vlog, total


def draft_direct(vin, vread, vwrite, vstep, rate, skip_x, lanes):
    _, vrun = draft_running(vstep, rate)
    scores = dot(vread, vwrite, NT)
    row = iota(vrun.shape, 0)
    pieces = []
    for j in range(DRAFT):
        gap = jnp.where(row >= j, vrun - vrun[j : j + 1, :], -jnp.inf)
        pieces.append(jnp.exp(gap) * vstep[j : j + 1, :] * scores[:, j : j + 1])
    pieces.append(jnp.exp(vrun))
    wide = spread(jnp.concatenate(pieces, axis=0), lanes)
    total = skip_x * vin
    for j in range(DRAFT):
        total = total + wide[j * DRAFT : (j + 1) * DRAFT, :] * vin[j : j + 1, :]
    return total, wide[DRAFT * DRAFT :, :]


def normed(y, vgate, gain):
    gated = y * (vgate / (1.0 + jnp.exp(-vgate)))
    mean = jnp.mean(gated * gated, axis=1, keepdims=True)
    return gated * lax.rsqrt(mean + EPSILON) * gain


IN_NAMES = 17


def mixer_kernel(nz, ny, nh, *refs):
    hbm, outs, vmem, scratch = (
        refs[:IN_NAMES],
        refs[IN_NAMES : IN_NAMES + 4],
        refs[IN_NAMES + 4 : 2 * IN_NAMES + 4],
        refs[2 * IN_NAMES + 4 :],
    )
    (
        x_ref,
        step_ref,
        w_ref,
        r_ref,
        rate_ref,
        skip_ref,
        res_ref,
        owner_ref,
        ids_ref,
        len_ref,
        di_ref,
        dg_ref,
        dw_ref,
        dr_ref,
        ds_ref,
        gain_ref,
        ow_ref,
    ) = vmem
    out_ref, ns_ref, vo_ref, ps_ref = outs
    (
        intra,
        decay_sq,
        lgp_send,
        lgp_recv,
        ls,
        ls_in,
        st_send,
        st_recv,
        en_send,
        en_recv,
        ent,
        ent_out,
        fin,
        fin32,
        pk,
        pk_pair,
        pky,
        pkz,
        pkf,
        pkf_own,
        pkf_other,
        own_a,
        own_b,
        ya,
        zb,
        ga,
        gb,
        ga_other,
        gb_other,
        part,
        total_ref,
        rs_send,
        rs_recv,
        fx_send,
        fx_recv,
        isem,
        sem,
        ysem,
        lsem,
        gsem,
        hsem,
    ) = scratch
    chips = nz * ny
    n = chips * CORES
    tile = HALF // chips
    me = lax.axis_index("seq")
    mh = lax.axis_index("head")
    core = me & 1
    chip = lax.shift_right_logical(me, 1)
    my_y = lax.rem(chip, ny)
    my_z = chip // ny
    pair = me + 1 - 2 * core
    is_low = core == 0

    def y_peer(k):
        return (my_z * ny + ((my_y + k) & (ny - 1))) * CORES + core

    def z_at(k):
        return ((my_z + k + nz) & (nz - 1))

    def z_peer(k):
        return (z_at(k) * ny + my_y) * CORES + core

    def push(src, dst, send, recv, peer, axis="seq"):
        pltpu.make_async_remote_copy(
            src_ref=src,
            dst_ref=dst,
            send_sem=send,
            recv_sem=recv,
            device_id={axis: peer},
            device_id_type=pl.DeviceIdType.MESH,
        ).start()

    def drain(ref, which):
        pltpu.make_async_copy(ref, ref, which).wait()

    sent = []

    for k in range(IN_NAMES):
        pltpu.make_async_copy(hbm[k], vmem[k], isem.at[k]).start()

    def load(*which):
        for k in which:
            pltpu.make_async_copy(hbm[k], vmem[k], isem.at[k]).wait()

    barrier = pltpu.get_barrier_semaphore()

    def greet(axis, peer):
        pl.semaphore_signal(
            barrier,
            inc=1,
            device_id={axis: peer},
            device_id_type=pl.DeviceIdType.MESH,
        )

    def greet_chip(k, _):
        greet("seq", ((chip + k) & (chips - 1)) * CORES + core)
        return 0

    def greet_head(k, _):
        greet("head", ((mh + k) & (nh - 1)))
        return 0

    greet("seq", pair)
    lax.fori_loop(1, chips, greet_chip, 0)
    lax.fori_loop(1, nh, greet_head, 0)

    lanes = head_lanes()
    square = (BLOCK, BLOCK)
    causal = iota(square, 0) >= iota(square, 1)
    tri = jnp.where(causal, 1.0, 0.0).astype(bf16)
    load(1, 4)
    rate = rate_ref[...]
    step_t = jnp.concatenate([step_ref[...], jnp.zeros((STATE - HEADS, BLOCK), f32)], axis=0)
    step = jnp.transpose(step_t)[:, 0:HEADS]
    logd = -(step * rate)
    running = sum(dot(tri, piece) for piece in reversed(parts(logd, 3)))
    last = running[BLOCK - 1 : BLOCK, :]
    lgp_send[...] = jnp.zeros((1, STATE), f32)
    lgp_send[:, 0:HEADS] = last
    to_end = jnp.exp(last - running) * step

    pl.semaphore_wait(barrier, chips + nh - 1)
    push(lgp_send, lgp_recv, sem.at[0], sem.at[1], pair)

    load(0, 2)
    weighted = (x_ref[...].astype(f32) * spread(to_end, lanes)).astype(bf16)
    ls[...] = dot(weighted, w_ref[...], TN)
    own_half = pl.ds(pl.multiple_of(core * HALF, HALF), HALF)
    pair_half = pl.ds(pl.multiple_of((1 - core) * HALF, HALF), HALF)
    push(ls.at[pair_half], ls_in, sem.at[2], sem.at[3], pair)

    load(5, 6, 7, 8, 9, 10, 11, 12, 13, 14, 15)
    owner = owner_ref[...]
    mine = owner == me
    mine_wide = jnp.broadcast_to(jnp.where(mine, 1.0, 0.0), (DRAFT, n))
    chosen = jnp.sum(mine_wide * ids_ref[...].astype(f32), axis=1, keepdims=True)
    candidates = di_ref.shape[0]
    pick = jnp.where(
        iota((DRAFT, candidates), 1) == chosen.astype(jnp.int32), 1.0, 0.0
    ).astype(bf16)
    vin = dot(pick, di_ref[...])
    vgate = dot(pick, dg_ref[...])
    vwrite = dot(pick, dw_ref[...])
    vread = dot(pick, dr_ref[...])
    vstep = sum(dot(pick, piece) for piece in reversed(parts(ds_ref[...], 3)))
    skip_x = spread(jnp.broadcast_to(skip_ref[...], (DRAFT, HEADS)), lanes)
    gain = gain_ref[...]
    direct, reach_x = draft_direct(
        vin, vread.astype(bf16), vwrite.astype(bf16), vstep, rate, skip_x, lanes
    )
    inter = dot(vread.astype(bf16), res_ref[...], NT)
    hidden = normed(direct + reach_x * inter, vgate, gain).astype(bf16)
    own_a[...] = hidden[:, :HALF]
    own_b[...] = hidden[:, HALF:]
    ya[my_y] = own_a[...]
    zb[my_z] = own_b[...]
    for k in range(1, ny):
        push(own_a, ya.at[my_y], gsem.at[0, k], gsem.at[0, 0], y_peer(k))
        sent.append((own_a, gsem.at[0, k]))
    for k in range(1, nz):
        push(own_b, zb.at[my_z], gsem.at[1, k], gsem.at[1, 0], z_peer(k))
        sent.append((own_b, gsem.at[1, k]))

    first = jnp.where(owner[:, 0:1] == me, 1.0, 0.0)
    step_high, step_low = parts(vstep, 2)
    blank = jnp.zeros((DRAFT, STATE - HEADS), f32)
    pk[...] = (
        jnp.concatenate(
            [
                jnp.concatenate([vin, vread, step_high.astype(f32), blank], axis=1),
                jnp.concatenate([vgate, vwrite, step_low.astype(f32), blank], axis=1),
            ],
            axis=0,
        )
        * first
    ).astype(bf16)
    push(pk, pk_pair, sem.at[6], sem.at[7], pair)

    sent.append((lgp_send, sem.at[0]))
    drain(lgp_recv, sem.at[1])
    own_log, other_log = lgp_send[...], lgp_recv[...]
    log_0 = jnp.where(is_low, own_log, other_log)
    log_1 = jnp.where(is_low, other_log, own_log)

    head_eye = iota((HEADS, STATE), 0) == iota((HEADS, STATE), 1)

    def head_rows(row):
        wide = jnp.where(head_eye, jnp.broadcast_to(row, (HEADS, STATE)), 0.0)
        return jnp.broadcast_to(jnp.sum(wide, axis=1, keepdims=True), (HEADS, STATE))

    def half_rows(row):
        wide = head_rows(row)
        return jnp.where(is_low, wide[0:HALF_HEADS, :], wide[HALF_HEADS:, :])

    decay_0, decay_1 = jnp.exp(half_rows(log_0)), jnp.exp(half_rows(log_1))
    chip_log = half_rows(own_log + other_log)
    log_rows = jnp.stack([piece.astype(f32) for piece in parts(chip_log, 3)], axis=1)
    log_rows = jnp.concatenate(
        [log_rows, jnp.zeros((HALF_HEADS, EXTRA - 3, STATE), f32)], axis=1
    )
    sharing = HEAD_DIM // tile
    log_rows = jnp.broadcast_to(log_rows[:, None], (HALF_HEADS, sharing, EXTRA, STATE))
    st_send[:, tile:, :] = log_rows.reshape(chips, EXTRA, STATE).astype(bf16)
    sent.append((ls_in, sem.at[2]))
    drain(ls_in, sem.at[3])
    own_rows, other_rows = ls[own_half, :], ls_in[...]
    state_0 = jnp.where(is_low, own_rows, other_rows)
    state_1 = jnp.where(is_low, other_rows, own_rows)
    ls_in[...] = state_0
    chip_state = jnp.concatenate(
        [
            state_0[h * HEAD_DIM : (h + 1) * HEAD_DIM, :] * decay_1[h : h + 1, :]
            + state_1[h * HEAD_DIM : (h + 1) * HEAD_DIM, :]
            for h in range(HALF_HEADS)
        ],
        axis=0,
    )
    st_send[:, 0:tile, :] = chip_state.astype(bf16).reshape(chips, tile, STATE)

    def send_states(k, _):
        to = ((chip + k * 13) & (chips - 1))
        push(st_send.at[to], st_recv.at[chip], sem.at[8], sem.at[9], to * CORES + core)
        return 0

    lax.fori_loop(1, chips, send_states, 0)
    st_recv[chip] = st_send[chip]

    sent.append((pk, sem.at[6]))
    drain(pk_pair, sem.at[7])
    chip_pack = (pk[...].astype(f32) + pk_pair[...].astype(f32)).astype(bf16)
    pky[my_y] = jnp.where(is_low, chip_pack[:, :PACK_HALF], chip_pack[:, PACK_HALF:])
    for k in range(1, ny):
        push(pky.at[my_y], pky.at[my_y], ysem.at[k], ysem.at[0], y_peer(k))
        sent.append((pky.at[my_y], ysem.at[k]))

    vlog, vrun = draft_running(vstep, rate)
    kept = jnp.sum(jnp.where(mine, len_ref[...], 0).astype(f32), axis=1, keepdims=True)
    live = iota(vlog.shape, 0).astype(f32) < kept
    reach = jnp.sum(jnp.where(live, vlog, 0.0), axis=0, keepdims=True)
    tail = jnp.exp(jnp.where(live, reach - vrun, -jnp.inf)) * vstep
    rows_keep = vin * spread(tail, lanes)
    high, low = parts(rows_keep, 2)
    twice = jnp.concatenate([high.astype(f32), low.astype(f32)], axis=0).astype(bf16)
    write_twice = jnp.concatenate([vwrite, vwrite], axis=0).astype(bf16)
    reach_rows = head_rows(
        jnp.concatenate([jnp.exp(reach), jnp.zeros((1, STATE - HEADS), f32)], axis=1)
    )

    drain(ya.at[pl.ds(0, ny - 1)], gsem.at[0, 0])
    drain(zb.at[pl.ds(0, nz - 1)], gsem.at[1, 0])
    ga[my_z] = ya[...]
    gb[my_y] = zb[...]
    for k in range(1, nz):
        push(ya, ga.at[my_z], gsem.at[2, k], gsem.at[2, 0], z_peer(k))
        sent.append((ya, gsem.at[2, k]))
    for k in range(1, ny):
        push(zb, gb.at[my_y], gsem.at[3, k], gsem.at[3, 0], y_peer(k))
        sent.append((zb, gsem.at[3, k]))

    drain(pky.at[pl.ds(0, ny - 1)], ysem.at[0])
    pkf[...] = jnp.sum(pky[...].astype(f32), axis=0).astype(bf16)
    pkz[my_z] = pkf[...]
    for k in range(1, nz):
        push(pkf, pkz.at[my_z], lsem.at[k], lsem.at[0], z_peer(k))
        sent.append((pkf, lsem.at[k]))

    drain(st_recv.at[pl.ds(0, chips - 1)], sem.at[9])
    sent.append((st_send.at[pl.ds(0, chips - 1)], sem.at[8]))
    logs = jnp.sum(st_recv[:, tile:, :].astype(f32), axis=1)
    decay_sq[...] = jnp.exp(logs)

    def scan_block(j, state):
        en_send[j, 0] = state.astype(bf16)
        return state * decay_sq[pl.ds(j, 1), :] + st_recv[j, 0:tile, :].astype(f32)

    final = lax.fori_loop(0, chips, scan_block, jnp.zeros((tile, STATE), f32)).astype(bf16)
    en_send[:, 1] = jnp.broadcast_to(final[None], (chips, tile, STATE))

    def send_entering(k, _):
        to = ((chip + k * 13) & (chips - 1))
        push(en_send.at[to], en_recv.at[chip], sem.at[10], sem.at[11], to * CORES + core)
        return 0

    lax.fori_loop(1, chips, send_entering, 0)
    en_recv[chip] = en_send[chip]

    load(3)
    scores = jnp.where(causal, dot(r_ref[...], w_ref[...], NT), 0.0)
    lanes128 = iota((BLOCK, STATE), 1)
    wide_run = jnp.concatenate([running, jnp.zeros((BLOCK, STATE - HEADS), f32)], axis=1)
    run_t = jnp.transpose(wide_run)

    for two in range(HALF_HEADS):
        columns = pl.ds(two * STATE, STATE)
        pair_x = x_ref[:, columns]
        sides = []
        for h in (2 * two, 2 * two + 1):
            gap = running[:, h : h + 1] - run_t[h : h + 1, :]
            decayed = jnp.exp(jnp.where(causal, gap, -jnp.inf))
            mixing = (scores * decayed * step_t[h : h + 1, :]).astype(bf16)
            sides.append(dot(mixing, pair_x))
        intra[:, columns] = jnp.where(lanes128 < HEAD_DIM, sides[0], sides[1])
    exp_x = spread(jnp.exp(running), lanes)

    drain(ga.at[pl.ds(0, nz - 1)], gsem.at[2, 0])
    push(ga, ga_other, sem.at[16], sem.at[17], pair)
    drain(gb.at[pl.ds(0, ny - 1)], gsem.at[3, 0])
    push(gb, gb_other, sem.at[18], sem.at[19], pair)
    drain(pkz.at[pl.ds(0, nz - 1)], lsem.at[0])
    pack_mine = jnp.sum(pkz[...].astype(f32), axis=0).astype(bf16)
    pkf_own[...] = pack_mine
    push(pkf_own, pkf_other, sem.at[20], sem.at[21], pair)
    sent.extend([(ga, sem.at[16]), (gb, sem.at[18]), (pkf_own, sem.at[20])])

    load(16)
    rows = n * DRAFT
    weight_a, weight_b = ow_ref[0:HALF, :], ow_ref[HALF:, :]

    def share(part_a, part_b):
        from_a = dot(part_a[...].reshape(rows // 2, HALF), weight_a)
        from_b = dot(part_b[...].reshape(rows // 2, HALF), weight_b)
        from_b = from_b.reshape(ny, nz, DRAFT, STATE)
        from_b = jnp.stack([from_b[k] for k in range(ny)], axis=1)
        return from_a.reshape(nz, ny, DRAFT, STATE) + from_b

    part[:, :, core] = share(ga, gb)

    drain(en_recv.at[pl.ds(0, chips - 1)], sem.at[11])
    sent.append((en_send.at[pl.ds(0, chips - 1)], sem.at[10]))
    fin[own_half, :] = en_recv[:, 1].reshape(HALF, STATE)
    push(fin.at[own_half], fin.at[own_half], sem.at[12], sem.at[13], pair)
    enter_0 = en_recv[:, 0].reshape(HALF, STATE)
    enter_1 = jnp.concatenate(
        [
            enter_0[h * HEAD_DIM : (h + 1) * HEAD_DIM, :].astype(f32) * decay_0[h : h + 1, :]
            + ls_in[h * HEAD_DIM : (h + 1) * HEAD_DIM, :]
            for h in range(HALF_HEADS)
        ],
        axis=0,
    ).astype(bf16)
    ent_out[...] = jnp.where(is_low, enter_1, enter_0)
    push(ent_out, ent.at[own_half], sem.at[14], sem.at[15], pair)
    ent[own_half, :] = jnp.where(is_low, enter_0, enter_1)

    drain(ga, sem.at[17])
    drain(gb, sem.at[19])
    part[:, :, 1 - core] = share(ga_other, gb_other)
    block_rows = rows // nh
    full = part[...].reshape(nh, block_rows, STATE)
    total_ref[...] = full
    rs_send[...] = full.astype(bf16)
    for k in range(1, nh):
        peer = ((mh + k) & (nh - 1))
        push(rs_send.at[peer], rs_recv.at[mh], hsem.at[0, k], hsem.at[0, 0], peer, "head")
        sent.append((rs_send.at[0], hsem.at[0, k]))
    rs_recv[mh] = jnp.zeros((block_rows, STATE), bf16)

    drain(pkf_other, sem.at[21])
    pack_mine = pack_mine.astype(f32)
    pack_other = pkf_other[...].astype(f32)
    pack_low = jnp.where(is_low, pack_mine, pack_other)
    pack_high = jnp.where(is_low, pack_other, pack_mine)
    pack = jnp.concatenate([pack_low, pack_high], axis=1)
    pin, pgate = pack[0:DRAFT, 0:WIDTH], pack[DRAFT:, 0:WIDTH]
    pread = pack[0:DRAFT, WIDTH : WIDTH + STATE].astype(bf16)
    pwrite = pack[DRAFT:, WIDTH : WIDTH + STATE].astype(bf16)
    pstep = (pack[0:DRAFT, WIDTH + STATE :] + pack[DRAFT:, WIDTH + STATE :])[:, 0:HEADS]
    pdirect, preach = draft_direct(pin, pread, pwrite, pstep, rate, skip_x, lanes)

    sent.append((ent_out, sem.at[12]))
    drain(ent_out, sem.at[13])
    phidden = normed(pdirect + preach * dot(pread, fin[...], NT), pgate, gain).astype(bf16)
    fix = dot(phidden, ow_ref[...])
    fx_send[...] = fix
    for k in range(1, nh):
        peer = ((mh + k) & (nh - 1))
        push(fx_send, fx_recv.at[mh], hsem.at[1, k], hsem.at[1, 0], peer, "head")
        sent.append((fx_send, hsem.at[1, k]))
    fx_recv[mh] = fix

    sent.append((ent_out, sem.at[14]))
    drain(ent_out, sem.at[15])
    inter_part = dot(r_ref[...], ent[...], NT) * exp_x
    out_ref[...] = (
        intra[...] + inter_part + skip_x[0:1, :] * x_ref[...].astype(f32)
    ).astype(bf16)

    fin32[...] = fin[...].astype(f32)
    pieces = HEAD_DIM // n
    for k in range(pieces):
        rows_at = pl.ds(me * pieces + k, HEADS, stride=HEAD_DIM)
        ps_ref[:, k * STATE : (k + 1) * STATE] = fin32[rows_at, :].astype(bf16)
    added = dot(twice, write_twice, TN)
    from_prompt = jnp.broadcast_to(first, (HEAD_DIM, STATE)) > 0.5
    for h in range(HEADS):
        span = slice(h * HEAD_DIM, (h + 1) * HEAD_DIM)
        start = jnp.where(from_prompt, fin32[span, :], res_ref[span, :].astype(f32))
        ns_ref[span, :] = (start * reach_rows[h : h + 1, :] + added[span, :]).astype(bf16)

    if nh > 1:
        drain(rs_recv.at[pl.ds(0, nh - 1)], hsem.at[0, 0])
        drain(fx_recv.at[pl.ds(0, nh - 1)], hsem.at[1, 0])
    total = total_ref[mh] + jnp.sum(rs_recv[...].astype(f32), axis=0)
    slots = block_rows // DRAFT
    fixed = jnp.concatenate([jnp.sum(fx_recv[...], axis=0)] * slots, axis=0)
    slot = mh * slots + lax.shift_right_logical(iota(total.shape, 0), 3)
    is_prompt = slot == jnp.broadcast_to(owner[:, 0:1], total.shape)
    vo_ref[...] = jnp.where(is_prompt, fixed, total).astype(bf16)
    for ref, which in sent:
        drain(ref, which)


def store_kernel(*refs):
    copies = [pltpu.make_async_copy(refs[k], refs[4 + k], refs[8].at[k]) for k in range(4)]
    for copy in copies:
        copy.start()
    for copy in copies:
        copy.wait()


def solution(mesh, nz=8, ny=4):
    n, nh = mesh.shape["seq"], mesh.shape["head"]
    chips = n // CORES
    tile = HALF // chips
    rows = n * DRAFT

    def on_device(
        prefill_input,
        prefill_step,
        write_proj,
        read_proj,
        decay_rate,
        skip_gain,
        resident_state,
        owner_slot,
        draft_ids,
        accepted_len,
        draft_input,
        draft_gate,
        draft_write,
        draft_read,
        draft_step,
        norm_gain,
        out_weight,
    ):
        vmem = pl.BlockSpec(memory_space=pltpu.VMEM)
        stay = pl.BlockSpec(memory_space=pltpu.HBM)
        args = (
            prefill_input,
            prefill_step.T,
            write_proj,
            read_proj,
            decay_rate[None],
            skip_gain[None],
            resident_state.reshape(WIDTH, STATE),
            owner_slot[None],
            draft_ids.T,
            accepted_len[None],
            draft_input,
            draft_gate,
            draft_write,
            draft_read,
            draft_step,
            norm_gain[None],
            out_weight,
        )
        args = tuple(pltpu.with_memory_space_constraint(a, pltpu.HBM) for a in args)
        block_rows = rows // nh
        scratch = [pltpu.VMEM(arg.shape, arg.dtype) for arg in args] + [
            pltpu.VMEM((BLOCK, WIDTH), f32),
            pltpu.VMEM((chips, STATE), f32),
            pltpu.VMEM((1, STATE), f32),
            pltpu.VMEM((1, STATE), f32),
            pltpu.VMEM((WIDTH, STATE), f32),
            pltpu.VMEM((HALF, STATE), f32),
            pltpu.VMEM((chips, tile + EXTRA, STATE), bf16),
            pltpu.VMEM((chips, tile + EXTRA, STATE), bf16),
            pltpu.VMEM((chips, 2, tile, STATE), bf16),
            pltpu.VMEM((chips, 2, tile, STATE), bf16),
            pltpu.VMEM((WIDTH, STATE), bf16),
            pltpu.VMEM((HALF, STATE), bf16),
            pltpu.VMEM((WIDTH, STATE), bf16),
            pltpu.VMEM((WIDTH, STATE), f32),
            pltpu.VMEM((ROWS2, PACK), bf16),
            pltpu.VMEM((ROWS2, PACK), bf16),
            pltpu.VMEM((ny, ROWS2, PACK_HALF), bf16),
            pltpu.VMEM((nz, ROWS2, PACK_HALF), bf16),
            pltpu.VMEM((ROWS2, PACK_HALF), bf16),
            pltpu.VMEM((ROWS2, PACK_HALF), bf16),
            pltpu.VMEM((ROWS2, PACK_HALF), bf16),
            pltpu.VMEM((DRAFT, HALF), bf16),
            pltpu.VMEM((DRAFT, HALF), bf16),
            pltpu.VMEM((ny, DRAFT, HALF), bf16),
            pltpu.VMEM((nz, DRAFT, HALF), bf16),
            pltpu.VMEM((nz, ny, DRAFT, HALF), bf16),
            pltpu.VMEM((ny, nz, DRAFT, HALF), bf16),
            pltpu.VMEM((nz, ny, DRAFT, HALF), bf16),
            pltpu.VMEM((ny, nz, DRAFT, HALF), bf16),
            pltpu.VMEM((nz, ny, CORES, DRAFT, STATE), f32),
            pltpu.VMEM((nh, block_rows, STATE), f32),
            pltpu.VMEM((nh, block_rows, STATE), bf16),
            pltpu.VMEM((nh, block_rows, STATE), bf16),
            pltpu.VMEM((DRAFT, STATE), f32),
            pltpu.VMEM((nh, DRAFT, STATE), f32),
            pltpu.SemaphoreType.DMA((IN_NAMES,)),
            pltpu.SemaphoreType.DMA((22,)),
            pltpu.SemaphoreType.DMA((ny,)),
            pltpu.SemaphoreType.DMA((nz,)),
            pltpu.SemaphoreType.DMA((4, max(ny, nz))),
            pltpu.SemaphoreType.DMA((2, nh)),
        ]
        shapes = (
            jax.ShapeDtypeStruct((BLOCK, WIDTH), bf16),
            jax.ShapeDtypeStruct((WIDTH, STATE), bf16),
            jax.ShapeDtypeStruct((block_rows, STATE), bf16),
            jax.ShapeDtypeStruct((HEADS, HEAD_DIM * STATE // n), bf16),
        )
        results = pl.pallas_call(
            functools.partial(mixer_kernel, nz, ny, nh),
            out_shape=shapes,
            in_specs=[stay] * len(args),
            out_specs=(vmem,) * 4,
            scratch_shapes=scratch,
            compiler_params=pltpu.CompilerParams(
                collective_id=0, has_side_effects=True, vmem_limit_bytes=VMEM_LIMIT
            ),
        )(*args)
        prefill_out, new_state, verify_out, piece = pl.pallas_call(
            store_kernel,
            out_shape=shapes,
            in_specs=[stay] * 4,
            out_specs=(stay,) * 4,
            scratch_shapes=[pltpu.SemaphoreType.DMA((4,))],
            compiler_params=pltpu.CompilerParams(vmem_limit_bytes=VMEM_LIMIT),
        )(*results)
        new_state = new_state.reshape(1, HEADS, HEAD_DIM, STATE)
        return prefill_out, new_state, verify_out, piece

    both, head = P("seq", "head"), P("head")
    cached = P("seq", "head", None, None)
    return jax.shard_map(
        on_device,
        mesh=mesh,
        in_specs=(
            both,
            both,
            both,
            both,
            head,
            head,
            cached,
            P(),
            P(),
            P(),
            both,
            both,
            both,
            both,
            both,
            head,
            P("head", "seq"),
        ),
        out_specs=(both, cached, P("head", "seq"), P("head", "seq")),
        check_vma=False,
    )
```
